32 devices in a mesh: groups: 2 (over y), seq: 4 (over z), cell: 4 (over x, core).
Axes of the slice: x: 2, y: 2, z: 4, core: 2. Of those that a mesh axis runs over, the one named last changes fastest.
Arguments:
- dna_bases: int32 [65536], P(('groups', 'seq')), parts along dimension 0, may hold values from 0 to 3
- stem_weight: bfloat16 [512, 768], replicated, may hold values from -0.5 to 0.5
- conv_weight: bfloat16 [2, 384, 3, 768], P(None, 'cell'), may hold values from -0.125 to 0.125
- proj_weight: bfloat16 [2, 384, 768], P(None, 'cell'), may hold values from -0.3125 to 0.3125
- emission_head_weight: bfloat16 [32, 768, 128], P('cell'), may hold values from -0.046875 to 0.046875
- transitions: float32 [32, 128, 128], P('cell'), may hold values from -1 to 109
Outputs:
- log_marginals: float32 [32, 512, 128], P('cell', ('groups', 'seq')), parts along dimension 1
The draws below stay inside these ranges and needn't reach their ends.
There are 2 independent parts, one for each index of `groups`. The reference program is written for one: setup_inputs(seed, part) draws one part's arguments, and reference() takes and returns one part's arrays. A program takes and returns all parts, laid end to end along the dimension named above; an argument that names none is the same for every part. Nothing has to cross between parts.
All inputs are finite; a program needn't handle non-finite values.
Results may differ from the reference program's by a relative error of at most 0.0007.
Values may be sent and summed in bfloat16 or wider, within the bound.
A program may use at most 128 MiB of HBM per device.

```python
import jax
import jax.numpy as jnp
from jax import lax

D = 768
INNER = 384
LABEL_COUNT = 128
TISSUE_TYPES = 32
BIN_BP = 128
LAYERS = 2
BASE_DILATION = 4
BINS = 256


def draw_transitions(key, part):
    noise_key = jax.random.fold_in(key, 7)
    persistence_random_seed = jax.random.fold_in(key, 13)
    cross_label_mask = jax.random.uniform(noise_key, (TISSUE_TYPES, LABEL_COUNT, LABEL_COUNT), jnp.float32, -1.0, 1.0)
    persistence_reward = jax.random.uniform(persistence_random_seed, (TISSUE_TYPES, 1, 1), jnp.float32, 8.0, 14.0)
    return cross_label_mask + persistence_reward * jnp.eye(LABEL_COUNT, dtype=jnp.float32)


def place_ends(values, stream_key, low, top_value):
    extent = values.shape
    place = [jax.random.randint(jax.random.fold_in(stream_key, axis), (), 0, extent[axis]) for axis in range(len(extent))]
    values = values.at[tuple(place)].set(low)
    longest = extent.index(max(extent))
    place[longest] = (place[longest] + 1) % extent[longest]
    return values.at[tuple(place)].set(top_value)


def shard_levels(key, extent, shards, smallest, top_value):
    def one(dim, shards_of):
        draws = jax.random.uniform(jax.random.fold_in(jax.random.fold_in(key, 6), dim), (shards_of,), jnp.float32, smallest / len(shards), top_value / len(shards))
        return jnp.repeat(jnp.exp(draws), extent[dim] // shards_of).reshape((-1,) + (1,) * (len(extent) - dim - 1))

    level = one(*shards[0])
    for cut in shards[1:]:
        level = level * one(*cut)
    return level


def noise(stream_key, extent, scale, limit, split=(), held_as=jnp.bfloat16):
    array = jax.random.normal(stream_key, extent, jnp.float32) * scale
    if len(split) > 0:
        array = shard_levels(stream_key, extent, split, -0.22, 0.18) * array
    return jnp.clip(array, min=-limit, max=limit).astype(held_as)


def setup_inputs(seed: int = 0, part: int = 0) -> dict:
    arg_keys = jax.random.split(jax.random.key(seed), 7)
    own_keys = jax.random.split(jax.random.fold_in(arg_keys[6], part), 7)
    return {
        "dna_bases": place_ends(jax.random.randint(own_keys[0], (BINS * BIN_BP,), 0, 4), jax.random.fold_in(own_keys[0], 1), 0, 3).astype(jnp.int32),
        "stem_weight": noise(arg_keys[1], (BIN_BP * 4, D), BIN_BP ** -0.5, 0.5),
        "conv_weight": noise(arg_keys[2], (LAYERS, INNER, 3, D), (3 * D) ** -0.5, 0.125, ((1, 4),)),
        "proj_weight": noise(arg_keys[3], (LAYERS, INNER, D), INNER ** -0.5, 0.3125, ((1, 4),)),
        "emission_head_weight": noise(arg_keys[4], (TISSUE_TYPES, D, LABEL_COUNT), (25 * D) ** -0.5, 0.046875, ((0, 4),)),
        "transitions": draw_transitions(jax.random.fold_in(arg_keys[6], 71), part),
    }


def scaled(values):
    return values * lax.rsqrt(lax.optimization_barrier(jnp.mean(values * values, axis=-1, keepdims=True)) + 1e-06)

def reference(dna_bases, stem_weight, conv_weight, proj_weight, emission_head_weight, transitions):
    base_hits = dna_bases.reshape(BINS, BIN_BP, 1) == jnp.arange(4, dtype=jnp.int32)
    one_hot = base_hits.astype(jnp.bfloat16).reshape(BINS, BIN_BP * 4)
    stem_out = jnp.dot(one_hot, stem_weight, preferred_element_type=jnp.float32).astype(jnp.bfloat16)
    residual = stem_out.astype(jnp.float32)
    for layer_position in range(LAYERS):
        spacing_multiplier = BASE_DILATION * 2 ** layer_position
        conv_input = jax.nn.gelu(scaled(residual)).astype(jnp.bfloat16)
        padded = jnp.pad(conv_input, ((spacing_multiplier, spacing_multiplier), (0, 0)))
        stacked = jnp.concatenate([padded[0:BINS], padded[spacing_multiplier:spacing_multiplier + BINS], padded[2 * spacing_multiplier:2 * spacing_multiplier + BINS]], axis=1)
        flat_weight = conv_weight[layer_position].reshape(INNER, 3 * D)
        conv_out = jnp.dot(stacked, flat_weight.T, preferred_element_type=jnp.float32)
        hidden = jax.nn.gelu(conv_out).astype(jnp.bfloat16)
        residual = residual + jnp.dot(hidden, proj_weight[layer_position], preferred_element_type=jnp.float32)
    trunk_features = scaled(residual).astype(jnp.bfloat16)
    emission_scores = jnp.einsum('aw,kwe->ake', trunk_features.astype(jnp.float32), emission_head_weight.astype(jnp.float32))

    def forward_step(carry_vec, emit_row):
        updated = emit_row + jax.nn.logsumexp(carry_vec[:, :, None] + transitions, axis=1)
        updated = updated - lax.optimization_barrier(jnp.max(updated, axis=1, keepdims=True))
        return (updated, updated)

    def backward_step(carry_vec, emit_row):
        earlier = jax.nn.logsumexp(transitions + (emit_row + carry_vec)[:, None, :], axis=2)
        earlier = earlier - lax.optimization_barrier(jnp.max(earlier, axis=1, keepdims=True))
        return (earlier, carry_vec)
    start_vec = jnp.zeros((TISSUE_TYPES, LABEL_COUNT), jnp.float32)
    _, alpha_all = lax.scan(forward_step, start_vec, emission_scores)
    _, beta_all = lax.scan(backward_step, start_vec, emission_scores, reverse=True)
    joint_log = alpha_all + beta_all
    result = jnp.maximum(joint_log - jax.nn.logsumexp(joint_log, axis=2, keepdims=True), -30.0)
    return jnp.transpose(result, (1, 0, 2))
```

```python
import functools

import jax
import jax.numpy as jnp
from jax import lax
from jax.experimental import pallas as pl
from jax.experimental.pallas import tpu as pltpu
from jax.sharding import PartitionSpec as P

BIN_BP = 128
BASE_DILATION = 4
SUB = 8
HALO = 16
WIDTH = 4
VMEM_LIMIT = 63 << 20
MESH = pl.DeviceIdType.MESH
F32 = jnp.float32
BF16 = jnp.bfloat16


def halves(x):
    hi = x.astype(BF16).astype(F32)
    return hi, x - hi


def beside(x):
    hi, lo = halves(x)
    return jnp.concatenate([hi.astype(BF16), lo.astype(BF16)], axis=1)


def above(x):
    hi, lo = halves(x)
    return jnp.concatenate([hi, lo], axis=0).astype(BF16)


def row_times(stacked, pair):
    n = pair.shape[1] // 2
    y = jnp.dot(stacked, pair, preferred_element_type=F32)
    y = y[:, :n] + y[:, n:]
    half = y.shape[0] // 2
    return y[:half] + y[half:]


def row_times_t(stacked, pair):
    y = lax.dot_general(
        jnp.concatenate([stacked, stacked], axis=1),
        pair,
        (((1,), (1,)), ((), ())),
        preferred_element_type=F32,
    )
    half = y.shape[0] // 2
    return y[:half] + y[half:]


def unit_rows(v):
    return v / jnp.max(v, axis=-1, keepdims=True)


def top(x):
    return jnp.max(jnp.max(x, axis=-1, keepdims=True), axis=-2, keepdims=True)


def rms(v):
    return v * lax.rsqrt(jnp.mean(v * v, axis=-1, keepdims=True) + 1e-06)


def crf_kernel(
    bases_hbm, stem_hbm, conv_hbm, proj_hbm, head_hbm, trans_hbm, out_ref,
    bases_ref, stem_ref, conv_ref, proj_ref, head_ref, trans_ref, lsem,
    wide_ref, wts_ref, gath_ref, hs_sem, hr_sem, ws_sem, wr_sem, gs_sem, gr_sem, feat_ref,
    f_ref, trn_ref, pair_ref, flip_ref, tree_ref, vin, win, vgot, wgot, vout, wout, st_ref,
    af_ref, al_ref, be_ref, ssem, rsem,
):
    cells, states = head_ref.shape[0], head_ref.shape[2]
    bins = feat_ref.shape[0]
    layers = conv_ref.shape[0]
    count = bins // SUB
    rows_wide = bins + 2 * HALO
    n = lax.axis_size("seq")
    me = lax.axis_index("seq")
    cell = lax.axis_index("cell")
    near = cell + 1 - 2 * (cell % 2)
    far = (cell + 2) % 4
    diag = (near + 2) % 4
    peers = (None, near, far, diag)

    loads = [
        pltpu.make_async_copy(src, dst, lsem.at[i])
        for i, (src, dst) in enumerate(
            [
                (bases_hbm, bases_ref), (proj_hbm, proj_ref), (stem_hbm, stem_ref),
                (conv_hbm, conv_ref.at[:, :, pl.ds(0, conv_hbm.shape[2])]),
                (trans_hbm, trans_ref), (head_hbm, head_ref),
            ]
        )
    ]
    for load in loads:
        load.start()
    missing = conv_ref.shape[2] - conv_hbm.shape[2]
    if missing:
        conv_ref[:, :, pl.ds(conv_hbm.shape[2], missing), :] = jnp.zeros(
            (layers, conv_ref.shape[1], missing, conv_ref.shape[3]), BF16
        )

    barrier = pltpu.get_barrier_semaphore()
    for peer in peers[1:]:
        pl.semaphore_signal(barrier, inc=1, device_id={"cell": peer}, device_id_type=MESH)

    @pl.when(me > 0)
    def _():
        pl.semaphore_signal(barrier, inc=1, device_id={"seq": me - 1}, device_id_type=MESH)

    @pl.when(me < n - 1)
    def _():
        pl.semaphore_signal(barrier, inc=1, device_id={"seq": me + 1}, device_id_type=MESH)

    inner = jnp.logical_and(me > 0, me < n - 1)
    pl.semaphore_wait(barrier, jnp.where(inner, 5, 4 if n > 1 else 3))

    upward = pltpu.make_async_remote_copy(
        bases_ref.at[pl.ds(bins - HALO, HALO)], wide_ref.at[pl.ds(0, HALO)],
        hs_sem.at[0], hr_sem.at[0],
        device_id={"seq": jnp.minimum(me + 1, n - 1)}, device_id_type=MESH,
    )
    downward = pltpu.make_async_remote_copy(
        bases_ref.at[pl.ds(0, HALO)], wide_ref.at[pl.ds(HALO, HALO)],
        hs_sem.at[1], hr_sem.at[1],
        device_id={"seq": jnp.maximum(me - 1, 0)}, device_id_type=MESH,
    )

    loads[0].wait()

    @pl.when(me < n - 1)
    def _():
        upward.start()

    @pl.when(me > 0)
    def _():
        downward.start()

    def send_weight(layer, k):
        own = pl.ds(0, proj_ref.shape[1])
        source = wts_ref.at[layer, 2, own] if k == 3 else proj_ref.at[layer]
        return pltpu.make_async_remote_copy(
            source, wts_ref.at[layer, k, own], ws_sem.at[layer, k], wr_sem.at[layer, k],
            device_id={"cell": far if k == 2 else near}, device_id_type=MESH,
        )

    def send_hidden(layer, k):
        return pltpu.make_async_remote_copy(
            gath_ref.at[layer, 0], gath_ref.at[layer, k], gs_sem.at[layer, k],
            gr_sem.at[layer, k], device_id={"cell": peers[k]}, device_id_type=MESH,
        )

    loads[1].wait()
    for layer in range(layers):
        send_weight(layer, 2).start()
        send_weight(layer, 1).start()
    held, padded = proj_ref.shape[1], wts_ref.shape[2]
    for layer in range(layers):
        wts_ref[layer, 0, pl.ds(0, held), :] = proj_ref[layer]
        if padded > held:
            for k in range(4):
                wts_ref[layer, k, pl.ds(held, padded - held), :] = jnp.zeros(
                    (padded - held, wts_ref.shape[3]), BF16
                )

    def prepare(c, _):
        raw = trans_ref[c]
        t = jnp.exp(raw - top(raw))
        trn_ref[c] = t
        pair_ref[c] = beside(t)
        flip_ref[c] = beside(t.T)
        return 0

    loads[4].wait()
    lax.fori_loop(0, cells // 2, prepare, 0)

    columns = lax.broadcasted_iota(jnp.int32, (BIN_BP, 4 * BIN_BP), 1)
    spread = (columns // 4 == lax.broadcasted_iota(jnp.int32, columns.shape, 0)).astype(BF16)

    @pl.when(me > 0)
    def _():
        upward.wait_recv()

    @pl.when(me == 0)
    def _():
        wide_ref[pl.ds(0, HALO), :] = jnp.zeros((HALO, BIN_BP), jnp.int32)

    @pl.when(me < n - 1)
    def _():
        downward.wait_recv()

    @pl.when(me == n - 1)
    def _():
        wide_ref[pl.ds(HALO, HALO), :] = jnp.zeros((HALO, BIN_BP), jnp.int32)

    bases = jnp.concatenate(
        [wide_ref[pl.ds(0, HALO), :], bases_ref[...], wide_ref[pl.ds(HALO, HALO), :]], axis=0
    )
    repeated = jnp.dot(
        bases.astype(F32).astype(BF16), spread, preferred_element_type=F32
    )
    which = (lax.broadcasted_iota(jnp.int32, repeated.shape, 1) % 4).astype(F32)
    one_hot = jnp.where(repeated == which, 1.0, 0.0).astype(BF16)
    loads[2].wait()
    residual = jnp.dot(one_hot, stem_ref[...], preferred_element_type=F32).astype(BF16).astype(F32)
    place = lax.broadcasted_iota(jnp.int32, residual.shape, 0) + (me * bins - HALO)
    inside = jnp.logical_and(place >= 0, place < n * bins)
    loads[3].wait()
    for layer in range(layers):
        dilation = BASE_DILATION * 2**layer
        conv_in = jnp.where(inside, jax.nn.gelu(rms(residual)), 0.0).astype(BF16)
        taps = [
            lax.dot_general(
                conv_in, conv_ref[layer, k], (((1,), (1,)), ((), ())), preferred_element_type=F32
            )
            for k in range(3)
        ]
        conv_out = (
            pltpu.roll(taps[0], dilation, 0)
            + taps[1]
            + pltpu.roll(taps[2], rows_wide - dilation, 0)
        )
        gath_ref[layer, 0] = jax.nn.gelu(conv_out).astype(BF16)
        for k in (2, 3, 1):
            send_hidden(layer, k).start()
        send_weight(layer, 2).wait_recv()
        send_weight(layer, 3).start()
        if layer == 0:
            lax.fori_loop(cells // 2, cells, prepare, 0)
        for k in (1, 2, 3):
            if k != 2:
                send_weight(layer, k).wait_recv()
            send_hidden(layer, k).wait_recv()
        hidden = jnp.concatenate([gath_ref[layer, k] for k in range(4)], axis=1)
        residual = residual + jnp.dot(
            hidden,
            wts_ref[layer].reshape(4 * padded, wts_ref.shape[3]),
            preferred_element_type=F32,
        )
    feat_ref[...] = rms(residual[HALO : HALO + bins]).astype(BF16)
    loads[5].wait()

    def chain(i, _):
        group = [WIDTH * i + k for k in range(WIDTH)]
        scores = [jnp.dot(feat_ref[...], head_ref[c], preferred_element_type=F32) for c in group]
        for c, e in zip(group, scores):
            f_ref[c] = jnp.exp(e - jnp.max(e, axis=1, keepdims=True))
        twice = [jnp.concatenate([pair_ref[c], pair_ref[c]], axis=0) for c in group]
        xs = [
            trn_ref[c][None] * f_ref[c, pl.ds(0, count, stride=SUB), :][:, None, :] for c in group
        ]
        for j in range(1, SUB):
            for p, c in enumerate(group):
                x = xs[p]
                scale = 1.0 / top(x)
                g = f_ref[c, pl.ds(j, count, stride=SUB), :][:, None, :] * scale
                y = jnp.dot(
                    beside(x.reshape(count * states, states)),
                    twice[p],
                    preferred_element_type=F32,
                )
                xs[p] = (y[:, :states] + y[:, states:]).reshape(count, states, states) * g
        layers_of = []
        for p, c in enumerate(group):
            x = xs[p] * (1.0 / top(xs[p]))
            layers_of.append([beside(x[k]) for k in range(count)])
            for k in range(count):
                tree_ref[c, k] = layers_of[p][k]
        place = count
        while len(layers_of[0]) > 1:
            half = len(layers_of[0]) // 2
            for p, c in enumerate(group):
                nodes = layers_of[p]
                joined = []
                for k in range(half):
                    right = jnp.concatenate([nodes[2 * k + 1], nodes[2 * k + 1]], axis=0)
                    y = jnp.dot(nodes[2 * k], right, preferred_element_type=F32)
                    y = y[:, :states] + y[:, states:]
                    node = beside(y * (1.0 / top(y)))
                    tree_ref[c, place + k] = node
                    joined.append(node)
                layers_of[p] = joined
            place += half
        return 0

    lax.fori_loop(0, cells // WIDTH, chain, 0)

    rows = lax.broadcasted_iota(jnp.int32, (cells, states), 0)

    def through(v, node, times):
        stacked = above(v)
        out = jnp.zeros_like(v)
        for c in range(cells):
            out = jnp.where(rows == c, times(stacked, tree_ref[c, node]), out)
        return unit_rows(out)

    whole = 2 * count - 2

    def forward_carry():
        @pl.when(me == 0)
        def _():
            vin[...] = jnp.ones_like(vin)

        @pl.when(me > 0)
        def _():
            pltpu.make_async_remote_copy(
                vout, vgot, ssem.at[0], rsem.at[0], device_id={"seq": me - 1}, device_id_type=MESH
            ).wait_recv()
            vin[...] = vgot[...]

        @pl.when(me < n - 1)
        def _():
            vout[...] = through(vin[...], whole, row_times)
            pltpu.make_async_remote_copy(
                vout, vgot, ssem.at[0], rsem.at[0], device_id={"seq": me + 1}, device_id_type=MESH
            ).start()

    def backward_carry():
        @pl.when(me == n - 1)
        def _():
            win[...] = jnp.ones_like(win)

        @pl.when(me < n - 1)
        def _():
            pltpu.make_async_remote_copy(
                wout, wgot, ssem.at[1], rsem.at[1], device_id={"seq": me + 1}, device_id_type=MESH
            ).wait_recv()
            win[...] = wgot[...]

        @pl.when(me > 0)
        def _():
            wout[...] = through(win[...], whole, row_times_t)
            pltpu.make_async_remote_copy(
                wout, wgot, ssem.at[1], rsem.at[1], device_id={"seq": me - 1}, device_id_type=MESH
            ).start()

    if n > 1:
        @pl.when(2 * me < n)
        def _():
            forward_carry()
            backward_carry()

        @pl.when(2 * me >= n)
        def _():
            backward_carry()
            forward_carry()
    else:
        vin[...] = jnp.ones_like(vin)
        win[...] = jnp.ones_like(win)

    starts = {0: vin[...]}
    afters = {count - 1: win[...]}
    width = count // 2
    base = 2 * count - 4
    while width >= 1:
        for k in range(0, count, 2 * width):
            starts[k + width] = through(starts[k], base + k // width, row_times)
            end = k + 2 * width - 1
            afters[end - width] = through(afters[end], base + end // width, row_times_t)
        width //= 2
        if width:
            base -= count // width
    for k in range(count):
        st_ref[pl.ds(k * cells, cells), :] = starts[k]
        af_ref[pl.ds(k * cells, cells), :] = afters[k]

    ahead = [st_ref[pl.ds(c, count, stride=cells), :] for c in range(cells)]
    behind = [af_ref[pl.ds(c, count, stride=cells), :] for c in range(cells)]
    for j in range(SUB):
        i = SUB - 1 - j
        for c in range(cells):
            fj = f_ref[c, pl.ds(j, count, stride=SUB), :]
            v = row_times(above(ahead[c]), pair_ref[c]) * fj
            v = unit_rows(v)
            al_ref[c, pl.ds(j * count, count), :] = v
            ahead[c] = v
            be_ref[c, pl.ds(i * count, count), :] = behind[c]
            if i > 0:
                fi = f_ref[c, pl.ds(i, count, stride=SUB), :]
                behind[c] = unit_rows(row_times(above(behind[c] * fi), flip_ref[c]))
    for c in range(cells):
        joint = jnp.log(al_ref[c]) + jnp.log(be_ref[c])
        peak = jnp.max(joint, axis=1, keepdims=True)
        total = jnp.log(jnp.sum(jnp.exp(joint - peak), axis=1, keepdims=True))
        result = jnp.maximum(joint - peak - total, -30.0)
        for j in range(SUB):
            out_ref[c, pl.ds(j, count, stride=SUB), :] = result[j * count : (j + 1) * count]

    if n > 1:
        @pl.when(me < n - 1)
        def _():
            pltpu.make_async_remote_copy(
                vout, vgot, ssem.at[0], rsem.at[0], device_id={"seq": me + 1}, device_id_type=MESH
            ).wait_send()

        @pl.when(me > 0)
        def _():
            pltpu.make_async_remote_copy(
                wout, wgot, ssem.at[1], rsem.at[1], device_id={"seq": me - 1}, device_id_type=MESH
            ).wait_send()

    @pl.when(me < n - 1)
    def _():
        upward.wait_send()

    @pl.when(me > 0)
    def _():
        downward.wait_send()

    for layer in range(layers):
        for k in (1, 2, 3):
            send_weight(layer, k).wait_send()
            send_hidden(layer, k).wait_send()


def per_device(dna_bases, stem_weight, conv_weight, proj_weight, emission_head_weight, transitions):
    bins = dna_bases.shape[0] // BIN_BP
    cells, _, states = emission_head_weight.shape
    layers, held, taps, wide = conv_weight.shape
    inner = pl.cdiv(held, 128) * 128
    count = bins // SUB
    assert HALO >= BASE_DILATION * (2**layers - 1) and lax.axis_size("cell") == 4
    rows = bins + 2 * HALO
    vmem = pl.BlockSpec(memory_space=pltpu.VMEM)
    hbm = pl.BlockSpec(memory_space=pl.ANY)
    vec = pltpu.VMEM((cells, states), F32)
    dma = pltpu.SemaphoreType.DMA
    return pl.pallas_call(
        crf_kernel,
        name="crf",
        out_shape=jax.ShapeDtypeStruct((cells, bins, states), F32),
        in_specs=[hbm] * 6,
        out_specs=vmem,
        scratch_shapes=[
            pltpu.VMEM((bins, BIN_BP), jnp.int32),
            pltpu.VMEM(stem_weight.shape, BF16),
            pltpu.VMEM((layers, taps, inner, wide), BF16),
            pltpu.VMEM(proj_weight.shape, BF16),
            pltpu.VMEM(emission_head_weight.shape, BF16),
            pltpu.VMEM(transitions.shape, F32),
            dma((6,)),
            pltpu.VMEM((2 * HALO, BIN_BP), jnp.int32),
            pltpu.VMEM((layers, 4, inner, wide), BF16),
            pltpu.VMEM((layers, 4, rows, inner), BF16),
            dma((2,)), dma((2,)),
            dma((layers, 4)), dma((layers, 4)), dma((layers, 4)), dma((layers, 4)),
            pltpu.VMEM((bins, wide), BF16),
            pltpu.VMEM((cells, bins, states), F32),
            pltpu.VMEM((cells, states, states), F32),
            pltpu.VMEM((cells, states, 2 * states), BF16),
            pltpu.VMEM((cells, states, 2 * states), BF16),
            pltpu.VMEM((cells, 2 * count - 1, states, 2 * states), BF16),
            vec, vec, vec, vec, vec, vec,
            pltpu.VMEM((count * cells, states), F32),
            pltpu.VMEM((count * cells, states), F32),
            pltpu.VMEM((cells, bins, states), F32),
            pltpu.VMEM((cells, bins, states), F32),
            dma((2,)), dma((2,)),
        ],
        compiler_params=pltpu.CompilerParams(
            collective_id=1, has_side_effects=True, vmem_limit_bytes=VMEM_LIMIT
        ),
    )(
        dna_bases.reshape(bins, BIN_BP),
        stem_weight,
        conv_weight.transpose(0, 2, 1, 3),
        proj_weight,
        emission_head_weight,
        transitions,
    )


def solution(mesh):
    placed = (
        P(("groups", "seq")),
        P(),
        P(None, "cell", None, None),
        P(None, "cell", None),
        P("cell", None, None),
        P("cell", None, None),
    )
    return jax.shard_map(
        per_device,
        mesh=mesh,
        in_specs=placed,
        out_specs=P("cell", ("groups", "seq"), None),
        check_vma=False,
    )
```

```python
import functools

import jax
import jax.numpy as jnp
from jax import lax
from jax.experimental import pallas as pl
from jax.experimental.pallas import tpu as pltpu
from jax.sharding import PartitionSpec as P

BIN_BP = 128
BASE_DILATION = 4
SUB = 8
HALO = 16
MARGIN = 8
WIDTH = 2
VMEM_LIMIT = 54800 << 10
MESH = pl.DeviceIdType.MESH
F32 = jnp.float32
BF16 = jnp.bfloat16


def tops(x):
    m = jnp.max(x, axis=-2, keepdims=True)
    return wide_tops(m)


def wide_tops(m):
    half = m.shape[-1] // 2
    shape = m.shape[:-1] + (half,)
    left = jnp.max(m[..., :half], axis=-1, keepdims=True)
    right = jnp.max(m[..., half:], axis=-1, keepdims=True)
    return jnp.concatenate([jnp.broadcast_to(left, shape), jnp.broadcast_to(right, shape)], axis=-1)


def two_blocks(x):
    half = x.shape[1] // 2
    zero = jnp.zeros((x.shape[0], half), x.dtype)
    return jnp.concatenate(
        [
            jnp.concatenate([x[:, :half], zero], axis=1),
            jnp.concatenate([zero, x[:, half:]], axis=1),
        ],
        axis=0,
    )


def rms(v):
    return v * lax.rsqrt(jnp.mean(v * v, axis=-1, keepdims=True) + 1e-06)


def crf_kernel(
    bases_hbm, stem_hbm, conv_hbm, proj_hbm, head_hbm, trans_hbm, out_ref,
    bases_ref, stem_ref, conv_ref, head_ref, trans_ref, lsem,
    wide_ref, wts_ref, mine0, got0, mine1, got1,
    hs_sem, hr_sem, cs_sem, cr_sem, ws_sem, wr_sem, gs_sem, gr_sem, feat_ref,
    f_ref, trn_ref, off_ref, flip_ref, own_ref, peak_ref, tree_ref, diag_ref,
    root_ref, rown_ref, next_ref, nown_ref, ms_sem, mr_sem,
    vin, win, vgot, wgot, vout, wout, st_ref, af_ref, al_ref, be_ref, ssem, rsem,
):
    cells, states = head_ref.shape[0], head_ref.shape[2]
    bins = feat_ref.shape[0]
    layers, taps = conv_ref.shape[:2]
    held, padded, wide = conv_hbm.shape[2], conv_ref.shape[2], conv_ref.shape[3]
    count = bins // SUB
    n = lax.axis_size("seq")
    me = lax.axis_index("seq")
    cell = lax.axis_index("cell")
    near = cell + 1 - 2 * (cell % 2)
    far = (cell + 2) % 4
    diag = (near + 2) % 4
    first, second = pl.ds(0, held), pl.ds(held, held)

    pairs = [(bases_hbm, bases_ref)]
    pairs += [(proj_hbm.at[k], wts_ref.at[k, 0, first]) for k in range(layers)]
    pairs += [(conv_hbm.at[k], conv_ref.at[k, :, first]) for k in range(layers)]
    pairs += [(stem_hbm, stem_ref), (trans_hbm, trans_ref), (head_hbm, head_ref)]
    loads = [pltpu.make_async_copy(a, b, lsem.at[i]) for i, (a, b) in enumerate(pairs)]
    for load in loads:
        load.start()
    base_load, proj_loads, conv_loads = loads[0], loads[1 : layers + 1], loads[layers + 1 : -3]
    stem_load, trans_load, head_load = loads[-3:]

    barrier = pltpu.get_barrier_semaphore()
    for peer in (near, far, diag):
        pl.semaphore_signal(barrier, inc=1, device_id={"cell": peer}, device_id_type=MESH)
    for step in (-1, 1, -2, 2):

        @pl.when(jnp.logical_and(me + step >= 0, me + step < n))
        def _():
            pl.semaphore_signal(barrier, inc=1, device_id={"seq": me + step}, device_id_type=MESH)
            if step in (-1, 1):
                pl.semaphore_signal(
                    barrier, inc=1, device_id={"seq": me + step, "cell": near}, device_id_type=MESH
                )

    extra = padded - 2 * held
    if extra:
        for layer in range(layers):
            conv_ref[layer, :, pl.ds(2 * held, extra), :] = jnp.zeros((taps, extra, wide), BF16)
            wts_ref[layer, :, pl.ds(2 * held, extra), :] = jnp.zeros((2, extra, wide), BF16)
    base_load.wait()
    greeted = sum(
        jnp.where(jnp.logical_and(me + step >= 0, me + step < n), 3 - abs(step), 0)
        for step in (-1, 1, -2, 2)
    )
    pl.semaphore_wait(barrier, 3 + greeted)

    upward = pltpu.make_async_remote_copy(
        bases_ref.at[pl.ds(bins - HALO, HALO)], wide_ref.at[pl.ds(0, HALO)],
        hs_sem.at[0], hr_sem.at[0],
        device_id={"seq": jnp.minimum(me + 1, n - 1), "cell": near}, device_id_type=MESH,
    )
    downward = pltpu.make_async_remote_copy(
        bases_ref.at[pl.ds(0, HALO)], wide_ref.at[pl.ds(HALO, HALO)],
        hs_sem.at[1], hr_sem.at[1],
        device_id={"seq": jnp.maximum(me - 1, 0), "cell": near}, device_id_type=MESH,
    )

    @pl.when(me < n - 1)
    def _():
        upward.start()

    @pl.when(me > 0)
    def _():
        downward.start()

    def send_conv(layer):
        return pltpu.make_async_remote_copy(
            conv_ref.at[layer, :, first], conv_ref.at[layer, :, second],
            cs_sem.at[layer], cr_sem.at[layer],
            device_id={"cell": near}, device_id_type=MESH,
        )

    def send_weight(layer, k):
        source = wts_ref.at[layer, 1, second] if k == 2 else wts_ref.at[layer, 0, first]
        target = wts_ref.at[layer, 0 if k == 0 else 1, first if k == 2 else second]
        return pltpu.make_async_remote_copy(
            source, target, ws_sem.at[layer, k], wr_sem.at[layer, k],
            device_id={"cell": far if k == 1 else near}, device_id_type=MESH,
        )

    mine, got = (mine0, mine1), (got0, got1)

    def send_hidden(layer):
        return pltpu.make_async_remote_copy(
            mine[layer], got[layer], gs_sem.at[layer], gr_sem.at[layer],
            device_id={"cell": diag}, device_id_type=MESH,
        )

    for layer in range(layers):
        proj_loads[layer].wait()
        if layer == 0:
            send_weight(layer, 1).start()
        conv_loads[layer].wait()
        send_conv(layer).start()
        send_weight(layer, 0).start()

    states_sq = (states, 2 * states)
    eye = lax.broadcasted_iota(jnp.int32, states_sq, 0) == lax.broadcasted_iota(
        jnp.int32, states_sq, 1
    ) % states

    def prepare(p, _):
        raw = jnp.concatenate([trans_ref[2 * p], trans_ref[2 * p + 1]], axis=1)
        peak = jnp.max(raw, axis=0, keepdims=True)
        t = jnp.exp(raw - peak)
        off = jnp.where(eye, 0.0, t)
        peak_ref[p] = peak
        own_ref[p] = jnp.sum(jnp.where(eye, t, 0.0), axis=0, keepdims=True)
        trn_ref[p] = t
        off_ref[p] = off.astype(BF16)
        flip_ref[p] = jnp.concatenate([off[:, :states].T, off[:, states:].T], axis=1).astype(BF16)
        return 0

    trans_load.wait()
    lax.fori_loop(0, cells // 4, prepare, 0)

    columns = lax.broadcasted_iota(jnp.int32, (BIN_BP, 4 * BIN_BP), 1)
    spread = (columns // 4 == lax.broadcasted_iota(jnp.int32, columns.shape, 0)).astype(BF16)
    stem_load.wait()

    @pl.when(me > 0)
    def _():
        upward.wait_recv()

    @pl.when(me == 0)
    def _():
        wide_ref[pl.ds(0, HALO), :] = jnp.zeros((HALO, BIN_BP), jnp.int32)

    @pl.when(me < n - 1)
    def _():
        downward.wait_recv()

    @pl.when(me == n - 1)
    def _():
        wide_ref[pl.ds(HALO, HALO), :] = jnp.zeros((HALO, BIN_BP), jnp.int32)

    bases = jnp.concatenate(
        [wide_ref[pl.ds(0, HALO), :], bases_ref[...], wide_ref[pl.ds(HALO, HALO), :]], axis=0
    )
    repeated = jnp.dot(
        bases.astype(F32).astype(BF16), spread, preferred_element_type=F32
    )
    which = (lax.broadcasted_iota(jnp.int32, repeated.shape, 1) % 4).astype(F32)
    one_hot = jnp.where(repeated == which, 1.0, 0.0).astype(BF16)
    residual = jnp.dot(one_hot, stem_ref[...], preferred_element_type=F32).astype(BF16).astype(F32)
    for layer in range(layers):
        dilation = BASE_DILATION * 2**layer
        rows_in = residual.shape[0]
        place = lax.broadcasted_iota(jnp.int32, residual.shape, 0) + (
            me * bins - (rows_in - bins) // 2
        )
        inside = jnp.logical_and(place >= 0, place < n * bins)
        conv_in = jnp.where(inside, jax.nn.gelu(rms(residual)), 0.0).astype(BF16)
        send_conv(layer).wait_recv()
        tap = [
            lax.dot_general(
                conv_in, conv_ref[layer, k], (((1,), (1,)), ((), ())), preferred_element_type=F32
            )
            for k in range(taps)
        ]
        conv_out = (
            pltpu.roll(tap[0], dilation, 0) + tap[1] + pltpu.roll(tap[2], rows_in - dilation, 0)
        )[MARGIN : rows_in - MARGIN]
        hidden = jax.nn.gelu(conv_out).astype(BF16)
        mine[layer][...] = hidden
        send_hidden(layer).start()
        if layer + 1 < layers:
            send_weight(layer + 1, 1).start()
        send_weight(layer, 1).wait_recv()
        send_weight(layer, 2).start()
        send_weight(layer, 0).wait_recv()
        if layer == 0:
            lax.fori_loop(cells // 4, cells // 2, prepare, 0)
        send_weight(layer, 2).wait_recv()
        send_hidden(layer).wait_recv()
        residual = residual[MARGIN : rows_in - MARGIN] + jnp.dot(
            jnp.concatenate([hidden, got[layer][...]], axis=1),
            wts_ref[layer].reshape(2 * padded, wide),
            preferred_element_type=F32,
        )
    feat_ref[...] = rms(residual).astype(BF16)
    head_load.wait()

    even = me % 2 == 0
    gives = jnp.logical_or(
        jnp.logical_and(even, me >= 2), jnp.logical_and(jnp.logical_not(even), me <= n - 3)
    )
    takes = jnp.logical_or(
        jnp.logical_and(even, me <= n - 4), jnp.logical_and(jnp.logical_not(even), me >= 3)
    )
    beside = jnp.minimum(me + 1 - 2 * (me % 2), n - 1)
    groups = cells // 2 // WIDTH

    def send_root(i):
        part = pl.ds(i * WIDTH, WIDTH)
        return pltpu.make_async_remote_copy(
            root_ref.at[part], next_ref.at[part], ms_sem.at[i], mr_sem.at[i],
            device_id={"seq": beside}, device_id_type=MESH,
        )

    send_rown = pltpu.make_async_remote_copy(
        rown_ref, nown_ref, ms_sem.at[groups], mr_sem.at[groups],
        device_id={"seq": beside}, device_id_type=MESH,
    )

    def rates(p, j):
        return jnp.concatenate(
            [f_ref[2 * p + h, pl.ds(j, count, stride=SUB), :] for h in range(2)], axis=1
        )

    def chain(i, _):
        group = [WIDTH * i + k for k in range(WIDTH)]
        for p in group:
            weight = jnp.concatenate([head_ref[2 * p], head_ref[2 * p + 1]], axis=1)
            e = jnp.dot(feat_ref[...], weight, preferred_element_type=F32) + peak_ref[p]
            f = jnp.exp(e - wide_tops(e))
            f_ref[2 * p] = f[:, :states]
            f_ref[2 * p + 1] = f[:, states:]
        blocks = [two_blocks(off_ref[p]) for p in group]
        xs = [
            trn_ref[p][None] * rates(p, 0)[:, None, :] for p in group
        ]
        for j in range(1, SUB):
            for q, p in enumerate(group):
                x = xs[q]
                g = rates(p, j)
                if j % 2 == 0:
                    g = g * (1.0 / wide_tops(jnp.max(x, axis=1)))
                h = g * own_ref[p]
                y = jnp.dot(
                    x.astype(BF16).reshape(count * states, 2 * states),
                    blocks[q],
                    preferred_element_type=F32,
                ).reshape(x.shape)
                xs[q] = y * g[:, None, :] + x * h[:, None, :]
        nodes = [[(x[k], 1.0 / tops(x[k])) for k in range(count)] for x in xs]
        place = 0
        width = count
        while width:
            for q, p in enumerate(group):
                joined = []
                for k, (x, scale) in enumerate(nodes[q]):
                    if place == 0:
                        x, scale = x * scale, 1.0
                    off = jnp.where(eye, 0.0, x).astype(BF16)
                    own = jnp.sum(jnp.where(eye, x, 0.0), axis=0, keepdims=True)
                    for h in range(2):
                        half = slice(h * states, (h + 1) * states)
                        if width > 1:
                            tree_ref[p, place + k, h] = off[:, half]
                            diag_ref[place + k, pl.ds(2 * p + h, 1), :] = own[:, half]
                        else:
                            root_ref[p, h] = off[:, half]
                            rown_ref[pl.ds(2 * p + h, 1), :] = own[:, half]
                    if k % 2 == 0:
                        left, left_scale = x, scale
                    else:
                        y = jnp.dot(
                            left.astype(BF16), two_blocks(off), preferred_element_type=F32
                        )
                        joined.append((y + left * own) * (left_scale * scale))
                nodes[q] = [(y, 1.0 / tops(y)) for y in joined]
            place += width
            width //= 2

        @pl.when(gives)
        def _():
            send_root(i).start()

        return 0

    lax.fori_loop(0, groups, chain, 0)

    @pl.when(gives)
    def _():
        send_rown.start()

    rows = lax.broadcasted_iota(jnp.int32, (cells, states), 0)

    def through(v, mats, own, back):
        low = v.astype(BF16)
        out = v * own
        for p in range(cells // 2):
            if back:
                y = lax.dot_general(
                    low, mats[p].reshape(2 * states, states),
                    (((1,), (1,)), ((), ())), preferred_element_type=F32,
                )
            else:
                both = jnp.concatenate([mats[p, 0], mats[p, 1]], axis=1)
                y = jnp.dot(low, both, preferred_element_type=F32)
            out = out + jnp.where(rows == 2 * p, y[:, :states], 0.0)
            out = out + jnp.where(rows == 2 * p + 1, y[:, states:], 0.0)
        return out * (1.0 / jnp.max(v, axis=-1, keepdims=True))

    def carry(from_first, start, arrived, out, k, back):
        side = -1 if back else 1

        def send(step):
            to = jnp.clip(me + side * step, 0, n - 1)
            return pltpu.make_async_remote_copy(
                out, arrived, ssem.at[k, step - 1], rsem.at[k],
                device_id={"seq": to}, device_id_type=MESH,
            )

        odd = from_first % 2 == 1
        hops = jnp.logical_and(odd, from_first >= 3)
        sends = jnp.logical_and(jnp.logical_or(odd, from_first == 0), from_first < n - 1)
        twice = jnp.logical_and(odd, from_first < n - 2)

        def run():
            @pl.when(from_first == 0)
            def _():
                start[...] = jnp.ones_like(start)

            @pl.when(from_first > 0)
            def _():
                send(1).wait_recv()

            @pl.when(jnp.logical_and(from_first > 0, jnp.logical_not(hops)))
            def _():
                start[...] = arrived[...]

            @pl.when(hops)
            def _():
                lax.fori_loop(0, groups, lambda i, _: (send_root(i).wait_recv(), 0)[1], 0)
                send_rown.wait_recv()
                start[...] = through(arrived[...], next_ref, nown_ref[...], back)

            @pl.when(sends)
            def _():
                out[...] = through(start[...], root_ref, rown_ref[...], back)
                send(1).start()

            @pl.when(twice)
            def _():
                send(2).start()

        def finish():
            @pl.when(sends)
            def _():
                send(1).wait_send()

            @pl.when(twice)
            def _():
                send(2).wait_send()

        return run, finish

    forward, forward_end = carry(me, vin, vgot, vout, 0, False)
    backward, backward_end = carry(n - 1 - me, win, wgot, wout, 1, True)

    @pl.when(2 * me < n)
    def _():
        forward()
        backward()

    @pl.when(2 * me >= n)
    def _():
        backward()
        forward()

    def step_through(v, node, back):
        return through(v, tree_ref.at[:, node], diag_ref[node], back)

    starts = {0: vin[...]}
    afters = {count - 1: win[...]}
    width = count // 2
    base = 2 * count - 4
    while width >= 1:
        for k in range(0, count, 2 * width):
            starts[k + width] = step_through(starts[k], base + k // width, False)
            end = k + 2 * width - 1
            afters[end - width] = step_through(afters[end], base + end // width, True)
        width //= 2
        if width:
            base -= count // width
    for k in range(count):
        st_ref[pl.ds(k * cells, cells), :] = starts[k]
        af_ref[pl.ds(k * cells, cells), :] = afters[k]

    def paired(ref, p):
        return jnp.concatenate(
            [ref[pl.ds(2 * p + h, count, stride=cells), :] for h in range(2)], axis=1
        )

    def advance(v, ref, p):
        stacked = jnp.concatenate([v[:, :states], v[:, states:]], axis=0).astype(BF16)
        y = jnp.dot(stacked, ref[p], preferred_element_type=F32)
        y = jnp.concatenate([y[:count, :states], y[count:, states:]], axis=1)
        return y + v * own_ref[p]

    ahead = [paired(st_ref, p) for p in range(cells // 2)]
    behind = [paired(af_ref, p) for p in range(cells // 2)]
    for j in range(SUB):
        i = SUB - 1 - j
        for p in range(cells // 2):
            v = ahead[p]
            fj = rates(p, j) * (1.0 / wide_tops(v))
            v = advance(v, off_ref, p) * fj
            al_ref[p, pl.ds(j * count, count), :] = v
            ahead[p] = v
            w = behind[p]
            be_ref[p, pl.ds(i * count, count), :] = w
            if i > 0:
                fi = rates(p, i) * (1.0 / wide_tops(w))
                behind[p] = advance(w * fi, flip_ref, p)
    for c in range(cells):
        half = pl.ds((c % 2) * states, states)
        joint = jnp.log(al_ref[c // 2, :, half]) + jnp.log(be_ref[c // 2, :, half])
        peak = jnp.max(joint, axis=1, keepdims=True)
        total = jnp.log(jnp.sum(jnp.exp(joint - peak), axis=1, keepdims=True))
        result = jnp.maximum(joint - peak - total, -30.0)
        for j in range(SUB):
            out_ref[c, pl.ds(j, count, stride=SUB), :] = result[j * count : (j + 1) * count]

    forward_end()
    backward_end()

    @pl.when(gives)
    def _():
        lax.fori_loop(0, groups, lambda i, _: (send_root(i).wait_send(), 0)[1], 0)
        send_rown.wait_send()

    @pl.when(me < n - 1)
    def _():
        upward.wait_send()

    @pl.when(me > 0)
    def _():
        downward.wait_send()

    for layer in range(layers):
        send_conv(layer).wait_send()
        send_hidden(layer).wait_send()
        for k in range(3):
            send_weight(layer, k).wait_send()


def per_device(dna_bases, stem_weight, conv_weight, proj_weight, emission_head_weight, transitions):
    bins = dna_bases.shape[0] // BIN_BP
    cells, _, states = emission_head_weight.shape
    layers, held, taps, wide = conv_weight.shape
    padded = pl.cdiv(2 * held, 256) * 256
    count = bins // SUB
    groups = cells // 2 // WIDTH
    n = lax.axis_size("seq")
    assert layers == 2 and HALO == layers * MARGIN and MARGIN >= BASE_DILATION * 2 ** (layers - 1)
    assert lax.axis_size("cell") == 4 and cells % (2 * WIDTH) == 0 and (n == 1 or n % 2 == 0)
    vmem = pl.BlockSpec(memory_space=pltpu.VMEM)
    hbm = pl.BlockSpec(memory_space=pl.ANY)
    vec = pltpu.VMEM((cells, states), F32)
    dma = pltpu.SemaphoreType.DMA
    square = (cells // 2, states, 2 * states)
    row = (cells // 2, 1, 2 * states)
    hidden = [pltpu.VMEM((bins + 2 * (HALO - (k + 1) * MARGIN), padded), BF16) for k in range(layers)]
    return pl.pallas_call(
        crf_kernel,
        name="crf",
        out_shape=jax.ShapeDtypeStruct((cells, bins, states), F32),
        in_specs=[hbm] * 6,
        out_specs=vmem,
        scratch_shapes=[
            pltpu.VMEM((bins, BIN_BP), jnp.int32),
            pltpu.VMEM(stem_weight.shape, BF16),
            pltpu.VMEM((layers, taps, padded, wide), BF16),
            pltpu.VMEM(emission_head_weight.shape, BF16),
            pltpu.VMEM(transitions.shape, F32),
            dma((2 * layers + 4,)),
            pltpu.VMEM((2 * HALO, BIN_BP), jnp.int32),
            pltpu.VMEM((layers, 2, padded, wide), BF16),
            hidden[0], hidden[0], hidden[1], hidden[1],
            dma((2,)), dma((2,)), dma((layers,)), dma((layers,)),
            dma((layers, 3)), dma((layers, 3)), dma((layers,)), dma((layers,)),
            pltpu.VMEM((bins, wide), BF16),
            pltpu.VMEM((cells, bins, states), F32),
            pltpu.VMEM(square, F32),
            pltpu.VMEM(square, BF16),
            pltpu.VMEM(square, BF16),
            pltpu.VMEM(row, F32),
            pltpu.VMEM(row, F32),
            pltpu.VMEM((cells // 2, 2 * count - 2, 2, states, states), BF16),
            pltpu.VMEM((2 * count - 2, cells, states), F32),
            pltpu.VMEM((cells // 2, 2, states, states), BF16),
            vec,
            pltpu.VMEM((cells // 2, 2, states, states), BF16),
            vec,
            dma((groups + 1,)), dma((groups + 1,)),
            vec, vec, vec, vec, vec, vec,
            pltpu.VMEM((count * cells, states), F32),
            pltpu.VMEM((count * cells, states), F32),
            pltpu.VMEM((cells // 2, bins, 2 * states), F32),
            pltpu.VMEM((cells // 2, bins, 2 * states), F32),
            dma((2, 2)), dma((2,)),
        ],
        compiler_params=pltpu.CompilerParams(
            collective_id=1, has_side_effects=True, vmem_limit_bytes=VMEM_LIMIT
        ),
    )(
        dna_bases.reshape(bins, BIN_BP),
        stem_weight,
        conv_weight.transpose(0, 2, 1, 3),
        proj_weight,
        emission_head_weight,
        transitions,
    )


def solution(mesh):
    placed = (
        P(("groups", "seq")),
        P(),
        P(None, "cell", None, None),
        P(None, "cell", None),
        P("cell", None, None),
        P("cell", None, None),
    )
    return jax.shard_map(
        per_device,
        mesh=mesh,
        in_specs=placed,
        out_specs=P("cell", ("groups", "seq"), None),
        check_vma=False,
    )
```

```python
import functools

import jax
import jax.numpy as jnp
from jax import lax
from jax.experimental import pallas as pl
from jax.experimental.pallas import tpu as pltpu
from jax.sharding import PartitionSpec as P

BIN_BP = 128
BASE_DILATION = 4
SUB = 8
HALO = 16
MARGIN = 8
WIDTH = 2
CELLS = 8
VMEM_LIMIT = 54800 << 10
MESH = pl.DeviceIdType.MESH
F32 = jnp.float32
BF16 = jnp.bfloat16


def tops(x):
    m = jnp.max(x, axis=-2, keepdims=True)
    return wide_tops(m)


def wide_tops(m):
    half = m.shape[-1] // 2
    shape = m.shape[:-1] + (half,)
    left = jnp.max(m[..., :half], axis=-1, keepdims=True)
    right = jnp.max(m[..., half:], axis=-1, keepdims=True)
    return jnp.concatenate([jnp.broadcast_to(left, shape), jnp.broadcast_to(right, shape)], axis=-1)


def wide_sums(x):
    half = x.shape[-1] // 2
    shape = x.shape[:-1] + (half,)
    left = jnp.sum(x[..., :half], axis=-1, keepdims=True)
    right = jnp.sum(x[..., half:], axis=-1, keepdims=True)
    return jnp.concatenate([jnp.broadcast_to(left, shape), jnp.broadcast_to(right, shape)], axis=-1)


def two_blocks(x):
    half = x.shape[1] // 2
    zero = jnp.zeros((x.shape[0], half), x.dtype)
    return jnp.concatenate(
        [
            jnp.concatenate([x[:, :half], zero], axis=1),
            jnp.concatenate([zero, x[:, half:]], axis=1),
        ],
        axis=0,
    )


def rms(v):
    return v * lax.rsqrt(jnp.mean(v * v, axis=-1, keepdims=True) + 1e-06)


def crf_kernel(
    bases_hbm, stem_hbm, conv_hbm, proj_hbm, head_hbm, trans_hbm, out_ref,
    bases_ref, stem_ref, conv_ref, head_ref, trans_ref, lsem,
    wide_ref, wts_ref, mine0, got0, mine1, got1,
    hs_sem, hr_sem, cs_sem, cr_sem, ws_sem, wr_sem, gs_sem, gr_sem, feat_ref,
    f_ref, trn_ref, off_ref, flip_ref, own_ref, peak_ref, tree_ref, diag_ref,
    root_ref, rown_ref, next_ref, nown_ref, ms_sem, mr_sem,
    twin_ref, town_ref, xs_sem, xr_sem, relays, ls_sem, lr_sem,
    vin, win, vgot, wgot, vout, wout, st_ref, kept_ref, ssem, rsem,
):
    cells, states = head_ref.shape[0], head_ref.shape[2]
    bins = feat_ref.shape[0]
    layers, taps = conv_ref.shape[:2]
    held, padded, wide = conv_hbm.shape[2], conv_ref.shape[2], conv_ref.shape[3]
    count = bins // SUB
    n = lax.axis_size("seq")
    me = lax.axis_index("seq")
    cell = lax.axis_index("cell")
    near = cell + 1 - 2 * (cell % 2)
    far = (cell + 2) % 4
    diag = (near + 2) % 4
    first, second = pl.ds(0, held), pl.ds(held, held)

    pairs = [(bases_hbm, bases_ref)]
    pairs += [(proj_hbm.at[k], wts_ref.at[k, 0, first]) for k in range(layers)]
    pairs += [(conv_hbm.at[k], conv_ref.at[k, :, first]) for k in range(layers)]
    pairs += [(stem_hbm, stem_ref), (trans_hbm, trans_ref), (head_hbm, head_ref)]
    loads = [pltpu.make_async_copy(a, b, lsem.at[i]) for i, (a, b) in enumerate(pairs)]
    for load in loads:
        load.start()
    base_load, proj_loads, conv_loads = loads[0], loads[1 : layers + 1], loads[layers + 1 : -3]
    stem_load, trans_load, head_load = loads[-3:]

    barrier = pltpu.get_barrier_semaphore()
    for peer in (near, far, diag):
        pl.semaphore_signal(barrier, inc=1, device_id={"cell": peer}, device_id_type=MESH)
    for step in (-1, 1, -2, 2):

        @pl.when(jnp.logical_and(me + step >= 0, me + step < n))
        def _():
            pl.semaphore_signal(barrier, inc=1, device_id={"seq": me + step}, device_id_type=MESH)
            pl.semaphore_signal(
                barrier, inc=1, device_id={"seq": me + step, "cell": near}, device_id_type=MESH
            )

    extra = padded - 2 * held
    if extra:
        for layer in range(layers):
            conv_ref[layer, :, pl.ds(2 * held, extra), :] = jnp.zeros((taps, extra, wide), BF16)
            wts_ref[layer, :, pl.ds(2 * held, extra), :] = jnp.zeros((2, extra, wide), BF16)
    base_load.wait()
    greeted = sum(
        jnp.where(jnp.logical_and(me + step >= 0, me + step < n), 2, 0)
        for step in (-1, 1, -2, 2)
    )
    pl.semaphore_wait(barrier, 3 + greeted)

    upward = pltpu.make_async_remote_copy(
        bases_ref.at[pl.ds(bins - HALO, HALO)], wide_ref.at[pl.ds(0, HALO)],
        hs_sem.at[0], hr_sem.at[0],
        device_id={"seq": jnp.minimum(me + 1, n - 1), "cell": near}, device_id_type=MESH,
    )
    downward = pltpu.make_async_remote_copy(
        bases_ref.at[pl.ds(0, HALO)], wide_ref.at[pl.ds(HALO, HALO)],
        hs_sem.at[1], hr_sem.at[1],
        device_id={"seq": jnp.maximum(me - 1, 0), "cell": near}, device_id_type=MESH,
    )

    @pl.when(me < n - 1)
    def _():
        upward.start()

    @pl.when(me > 0)
    def _():
        downward.start()

    def send_conv(layer):
        return pltpu.make_async_remote_copy(
            conv_ref.at[layer, :, first], conv_ref.at[layer, :, second],
            cs_sem.at[layer], cr_sem.at[layer],
            device_id={"cell": near}, device_id_type=MESH,
        )

    def send_weight(layer, k):
        source = wts_ref.at[layer, 1, second] if k == 2 else wts_ref.at[layer, 0, first]
        target = wts_ref.at[layer, 0 if k == 0 else 1, first if k == 2 else second]
        return pltpu.make_async_remote_copy(
            source, target, ws_sem.at[layer, k], wr_sem.at[layer, k],
            device_id={"cell": far if k == 1 else near}, device_id_type=MESH,
        )

    mine, got = (mine0, mine1), (got0, got1)

    def send_hidden(layer):
        return pltpu.make_async_remote_copy(
            mine[layer], got[layer], gs_sem.at[layer], gr_sem.at[layer],
            device_id={"cell": diag}, device_id_type=MESH,
        )

    for layer in range(layers):
        proj_loads[layer].wait()
        if layer == 0:
            send_weight(layer, 1).start()
        conv_loads[layer].wait()
        send_conv(layer).start()
        send_weight(layer, 0).start()

    states_sq = (states, 2 * states)
    eye = lax.broadcasted_iota(jnp.int32, states_sq, 0) == lax.broadcasted_iota(
        jnp.int32, states_sq, 1
    ) % states

    def prepare(p, _):
        raw = jnp.concatenate([trans_ref[2 * p], trans_ref[2 * p + 1]], axis=1)
        peak = jnp.max(raw, axis=0, keepdims=True)
        t = jnp.exp(raw - peak)
        off = jnp.where(eye, 0.0, t)
        peak_ref[p] = peak
        own_ref[p] = jnp.sum(jnp.where(eye, t, 0.0), axis=0, keepdims=True)
        trn_ref[p] = t
        off_ref[p] = off.astype(BF16)
        flip_ref[p] = jnp.concatenate([off[:, :states].T, off[:, states:].T], axis=1).astype(BF16)
        return 0

    trans_load.wait()
    lax.fori_loop(0, cells // 4, prepare, 0)

    columns = lax.broadcasted_iota(jnp.int32, (BIN_BP, 4 * BIN_BP), 1)
    spread = (columns // 4 == lax.broadcasted_iota(jnp.int32, columns.shape, 0)).astype(BF16)
    stem_load.wait()

    @pl.when(me > 0)
    def _():
        upward.wait_recv()

    @pl.when(me == 0)
    def _():
        wide_ref[pl.ds(0, HALO), :] = jnp.zeros((HALO, BIN_BP), jnp.int32)

    @pl.when(me < n - 1)
    def _():
        downward.wait_recv()

    @pl.when(me == n - 1)
    def _():
        wide_ref[pl.ds(HALO, HALO), :] = jnp.zeros((HALO, BIN_BP), jnp.int32)

    bases = jnp.concatenate(
        [wide_ref[pl.ds(0, HALO), :], bases_ref[...], wide_ref[pl.ds(HALO, HALO), :]], axis=0
    )
    repeated = jnp.dot(
        bases.astype(F32).astype(BF16), spread, preferred_element_type=F32
    )
    which = (lax.broadcasted_iota(jnp.int32, repeated.shape, 1) % 4).astype(F32)
    one_hot = jnp.where(repeated == which, 1.0, 0.0).astype(BF16)
    residual = jnp.dot(one_hot, stem_ref[...], preferred_element_type=F32).astype(BF16).astype(F32)
    for layer in range(layers):
        dilation = BASE_DILATION * 2**layer
        rows_in = residual.shape[0]
        place = lax.broadcasted_iota(jnp.int32, residual.shape, 0) + (
            me * bins - (rows_in - bins) // 2
        )
        inside = jnp.logical_and(place >= 0, place < n * bins)
        conv_in = jnp.where(inside, jax.nn.gelu(rms(residual)), 0.0).astype(BF16)
        send_conv(layer).wait_recv()
        tap = [
            lax.dot_general(
                conv_in, conv_ref[layer, k], (((1,), (1,)), ((), ())), preferred_element_type=F32
            )
            for k in range(taps)
        ]
        conv_out = (
            pltpu.roll(tap[0], dilation, 0) + tap[1] + pltpu.roll(tap[2], rows_in - dilation, 0)
        )[MARGIN : rows_in - MARGIN]
        hidden = jax.nn.gelu(conv_out).astype(BF16)
        mine[layer][...] = hidden
        send_hidden(layer).start()
        if layer + 1 < layers:
            send_weight(layer + 1, 1).start()
        send_weight(layer, 1).wait_recv()
        send_weight(layer, 2).start()
        send_weight(layer, 0).wait_recv()
        if layer == 0:
            lax.fori_loop(cells // 4, cells // 2, prepare, 0)
        send_weight(layer, 2).wait_recv()
        send_hidden(layer).wait_recv()
        residual = residual[MARGIN : rows_in - MARGIN] + jnp.dot(
            jnp.concatenate([hidden, got[layer][...]], axis=1),
            wts_ref[layer].reshape(2 * padded, wide),
            preferred_element_type=F32,
        )
    feat_ref[...] = rms(residual).astype(BF16)
    head_load.wait()

    even = me % 2 == 0
    gives = jnp.logical_or(
        jnp.logical_and(even, me >= 2), jnp.logical_and(jnp.logical_not(even), me <= n - 3)
    )
    beside = jnp.minimum(me + 1 - 2 * (me % 2), n - 1)
    groups = cells // 2 // WIDTH

    def send_root(g):
        return [
            pltpu.make_async_remote_copy(
                a.at[g], b.at[g], ms_sem.at[g, i], mr_sem.at[g, i],
                device_id={"seq": beside}, device_id_type=MESH,
            )
            for i, (a, b) in enumerate([(root_ref, next_ref), (rown_ref, nown_ref)])
        ]

    swaps = jnp.logical_and(jnp.logical_or(me == 1, me == n - 2), n > 2)

    def send_near(g):
        return [
            pltpu.make_async_remote_copy(
                a.at[g], b.at[g], xs_sem.at[g, i], xr_sem.at[g, i],
                device_id={"cell": near}, device_id_type=MESH,
            )
            for i, (a, b) in enumerate([(root_ref, twin_ref), (rown_ref, town_ref)])
        ]

    def rates(p, j):
        return jnp.concatenate(
            [f_ref[2 * p + h, pl.ds(j, count, stride=SUB), :] for h in range(2)], axis=1
        )

    def chain(g):
        group = [WIDTH * g + q for q in range(WIDTH)]
        for p in group:
            weight = jnp.concatenate([head_ref[2 * p], head_ref[2 * p + 1]], axis=1)
            e = jnp.dot(feat_ref[...], weight, preferred_element_type=F32) + peak_ref[p]
            f = jnp.exp(e - wide_tops(e))
            f_ref[2 * p] = f[:, :states]
            f_ref[2 * p + 1] = f[:, states:]
        blocks = [two_blocks(off_ref[p]) for p in group]
        xs = [trn_ref[p][None] * rates(p, 0)[:, None, :] for p in group]
        scales = {}
        for j in range(1, SUB):
            for q, p in enumerate(group):
                x = xs[q]
                r = rates(p, j)
                if j == SUB // 2:
                    scales[q] = 1.0 / wide_tops(jnp.max(x, axis=1))
                if j == SUB // 2 + 1:
                    r = r * scales[q]
                h = r * own_ref[p]
                y = jnp.dot(
                    x.astype(BF16).reshape(count * states, 2 * states),
                    blocks[q],
                    preferred_element_type=F32,
                ).reshape(x.shape)
                xs[q] = y * r[:, None, :] + x * h[:, None, :]
        nodes = [[(x[k], None) for k in range(count)] for x in xs]
        place = 0
        width = count
        while width:
            for q in range(WIDTH):
                joined = []
                for k, (x, scale) in enumerate(nodes[q]):
                    slanted = jnp.where(eye, x, 0.0)
                    off = (x - slanted).astype(BF16)
                    own = jnp.sum(slanted, axis=0, keepdims=True)
                    for h in range(2):
                        half = slice(h * states, (h + 1) * states)
                        if width > 1:
                            tree_ref[g, place + k, q, h] = off[:, half]
                            diag_ref[g, place + k, pl.ds(2 * q + h, 1), :] = own[:, half]
                        else:
                            root_ref[g, q, h] = off[:, half]
                            rown_ref[g, pl.ds(2 * q + h, 1), :] = own[:, half]
                    if k % 2 == 0:
                        left, left_scale = x, scale
                    else:
                        y = jnp.dot(
                            left.astype(BF16), two_blocks(off), preferred_element_type=F32
                        )
                        y = y + left * own
                        joined.append(y if scale is None else y * (left_scale * scale))
                nodes[q] = [(y, 1.0 / tops(y)) for y in joined]
            place += width
            width //= 2

        @pl.when(swaps)
        def _():
            for copy in send_near(g):
                copy.start()

        @pl.when(gives)
        def _():
            for copy in send_root(g):
                copy.start()

    rows = lax.broadcasted_iota(jnp.int32, (CELLS, states), 0)

    def through(v, mats, own, back, level=True):
        low = v.astype(BF16)
        out = v * own
        for q in range(WIDTH):
            if back:
                y = lax.dot_general(
                    low, mats[q].reshape(2 * states, states),
                    (((1,), (1,)), ((), ())), preferred_element_type=F32,
                )
            else:
                both = jnp.concatenate([mats[q, 0], mats[q, 1]], axis=1)
                y = jnp.dot(low, both, preferred_element_type=F32)
            out = out + jnp.where(rows == 2 * q, y[:, :states], 0.0)
            out = out + jnp.where(rows == 2 * q + 1, y[:, states:], 0.0)
        return out * (1.0 / jnp.max(v, axis=-1, keepdims=True)) if level else out

    def carry(from_first, starts, arrivals, outs, k, back, g):
        side = -1 if back else 1
        start, arrived, out = starts.at[g], arrivals.at[g], outs.at[g]

        def send(step):
            to = jnp.clip(me + side * step, 0, n - 1)
            return pltpu.make_async_remote_copy(
                out, arrived, ssem.at[g, k, step - 1], rsem.at[g, k],
                device_id={"seq": to, "cell": jnp.where(from_first == 1, near, cell)},
                device_id_type=MESH,
            )

        relayed = relays.at[g, k]
        send_relay = pltpu.make_async_remote_copy(
            out, relayed, ls_sem.at[g, k], lr_sem.at[g, k],
            device_id={"seq": jnp.clip(me + side, 0, n - 1), "cell": near}, device_id_type=MESH,
        )
        odd = from_first % 2 == 1
        hops = jnp.logical_and(odd, from_first >= 3)
        sends = jnp.logical_and(hops, from_first < n - 1)
        turns = jnp.logical_and(from_first == 1, n > 2)
        twice = jnp.logical_and(odd, from_first < n - 2)

        def lead():
            @pl.when(from_first == 0)
            def _():
                start[...] = jnp.ones((CELLS, states), F32)

            @pl.when(jnp.logical_and(from_first == 0, n > 1))
            def _():
                out[...] = through(
                    jnp.ones((CELLS, states), F32), root_ref.at[g], rown_ref[g], back
                )
                if n > 2:
                    send_relay.start()
                send(1).start()

        def run():
            @pl.when(turns)
            def _():
                for copy in send_near(g):
                    copy.wait_recv()
                send_relay.wait_recv()
                out[...] = through(relayed[...], twin_ref.at[g], town_ref[g], back)
                send(2).start()
                send(1).start()

            @pl.when(from_first > 0)
            def _():
                send(1).wait_recv()

            @pl.when(jnp.logical_and(from_first > 0, jnp.logical_not(hops)))
            def _():
                start[...] = arrived[...]

            @pl.when(hops)
            def _():
                for copy in send_root(g):
                    copy.wait_recv()
                start[...] = through(arrived[...], next_ref.at[g], nown_ref[g], back)

            @pl.when(sends)
            def _():
                out[...] = through(start[...], root_ref.at[g], rown_ref[g], back)
                send(1).start()

            @pl.when(jnp.logical_and(twice, hops))
            def _():
                send(2).start()

        def finish():
            @pl.when(jnp.logical_or(jnp.logical_or(sends, turns), jnp.logical_and(from_first == 0, n > 1)))
            def _():
                send(1).wait_send()

            @pl.when(jnp.logical_and(from_first == 0, n > 2))
            def _():
                send_relay.wait_send()

            @pl.when(twice)
            def _():
                send(2).wait_send()

        return lead, run, finish

    def sweep(g, back, last):
        def step_through(v, node):
            return through(v, tree_ref.at[g, node], diag_ref[g, node], back, False)

        edge = count - 1 if back else 0
        chunk = {edge: win[g] if back else vin[g]}
        width = count // 2
        base = 2 * count - 4
        while width >= 1:
            for k in range(0, count, 2 * width):
                if back:
                    end = k + 2 * width - 1
                    chunk[end - width] = step_through(chunk[end], base + end // width)
                else:
                    chunk[k + width] = step_through(chunk[k], base + k // width)
            width //= 2
            if width:
                base -= count // width
        for k in range(count):
            st_ref[g, pl.ds(k * CELLS, CELLS), :] = chunk[k]

        def advance(v, ref, p):
            stacked = jnp.concatenate([v[:, :states], v[:, states:]], axis=0).astype(BF16)
            y = jnp.dot(stacked, ref[p], preferred_element_type=F32)
            y = jnp.concatenate([y[:count, :states], y[count:, states:]], axis=1)
            return y + v * own_ref[p]

        def emit(q, j, v):
            p = WIDTH * g + q
            joint = jnp.log(v) + kept_ref[p, j]
            joint = joint - wide_tops(joint)
            result = jnp.maximum(joint - jnp.log(wide_sums(jnp.exp(joint))), -30.0)
            for h in range(2):
                out_ref[2 * p + h, pl.ds(j, count, stride=SUB), :] = result[
                    :, h * states : (h + 1) * states
                ]

        state = [
            jnp.concatenate(
                [st_ref[g, pl.ds(2 * q + h, count, stride=CELLS), :] for h in range(2)], axis=1
            )
            for q in range(WIDTH)
        ]
        for step in range(SUB):
            j = SUB - 1 - step if back else step
            for q in range(WIDTH):
                p = WIDTH * g + q
                v = state[q]
                if not back or step < SUB - 1:
                    f = rates(p, j)
                    if step % (SUB // 2) == 0:
                        f = f * (1.0 / wide_tops(v))
                    if back:
                        state[q] = advance(v * f, flip_ref, p)
                    else:
                        state[q] = advance(v, off_ref, p) * f
                v = v if back else state[q]
                if last:
                    emit(q, j, v)
                else:
                    kept_ref[p, j] = jnp.log(v)

    rown_ref[...] = jnp.ones_like(rown_ref)
    diag_ref[...] = jnp.ones_like(diag_ref)
    carries = [
        (
            carry(me, vin, vgot, vout, 0, False, g),
            carry(n - 1 - me, win, wgot, wout, 1, True, g),
        )
        for g in range(groups)
    ]
    for g in range(groups):
        chain(g)
        for part in carries[g]:
            part[0]()
    early = 2 * me < n
    late = jnp.logical_not(early)
    for last in (False, True):
        for g in range(groups):
            for k, when in ((0, early), (1, late)):
                way = 1 - k if last else k

                @pl.when(when)
                def _():
                    carries[g][way][1]()
                    sweep(g, way == 1, last)

    for g in range(groups):
        for part in carries[g]:
            part[2]()

    @pl.when(swaps)
    def _():
        for g in range(groups):
            for copy in send_near(g):
                copy.wait_send()

    @pl.when(gives)
    def _():
        for g in range(groups):
            for copy in send_root(g):
                copy.wait_send()

    @pl.when(me < n - 1)
    def _():
        upward.wait_send()

    @pl.when(me > 0)
    def _():
        downward.wait_send()

    for layer in range(layers):
        send_conv(layer).wait_send()
        send_hidden(layer).wait_send()
        for k in range(3):
            send_weight(layer, k).wait_send()


def per_device(dna_bases, stem_weight, conv_weight, proj_weight, emission_head_weight, transitions):
    bins = dna_bases.shape[0] // BIN_BP
    cells, _, states = emission_head_weight.shape
    layers, held, taps, wide = conv_weight.shape
    padded = pl.cdiv(2 * held, 256) * 256
    count = bins // SUB
    groups = cells // 2 // WIDTH
    n = lax.axis_size("seq")
    assert layers == 2 and HALO == layers * MARGIN and MARGIN >= BASE_DILATION * 2 ** (layers - 1)
    assert lax.axis_size("cell") == 4 and 2 * WIDTH <= CELLS and cells % (2 * WIDTH) == 0 and (n == 1 or n % 2 == 0)
    vmem = pl.BlockSpec(memory_space=pltpu.VMEM)
    hbm = pl.BlockSpec(memory_space=pl.ANY)
    vec = pltpu.VMEM((groups, CELLS, states), F32)
    root = pltpu.VMEM((groups, WIDTH, 2, states, states), BF16)
    dma = pltpu.SemaphoreType.DMA
    square = (cells // 2, states, 2 * states)
    row = (cells // 2, 1, 2 * states)
    hidden = [pltpu.VMEM((bins + 2 * (HALO - (k + 1) * MARGIN), padded), BF16) for k in range(layers)]
    return pl.pallas_call(
        crf_kernel,
        name="crf",
        out_shape=jax.ShapeDtypeStruct((cells, bins, states), F32),
        in_specs=[hbm] * 6,
        out_specs=vmem,
        scratch_shapes=[
            pltpu.VMEM((bins, BIN_BP), jnp.int32),
            pltpu.VMEM(stem_weight.shape, BF16),
            pltpu.VMEM((layers, taps, padded, wide), BF16),
            pltpu.VMEM(emission_head_weight.shape, BF16),
            pltpu.VMEM(transitions.shape, F32),
            dma((2 * layers + 4,)),
            pltpu.VMEM((2 * HALO, BIN_BP), jnp.int32),
            pltpu.VMEM((layers, 2, padded, wide), BF16),
            hidden[0], hidden[0], hidden[1], hidden[1],
            dma((2,)), dma((2,)), dma((layers,)), dma((layers,)),
            dma((layers, 3)), dma((layers, 3)), dma((layers,)), dma((layers,)),
            pltpu.VMEM((bins, wide), BF16),
            pltpu.VMEM((cells, bins, states), F32),
            pltpu.VMEM(square, F32),
            pltpu.VMEM(square, BF16),
            pltpu.VMEM(square, BF16),
            pltpu.VMEM(row, F32),
            pltpu.VMEM(row, F32),
            pltpu.VMEM((groups, 2 * count - 2, WIDTH, 2, states, states), BF16),
            pltpu.VMEM((groups, 2 * count - 2, CELLS, states), F32),
            root, vec, root, vec,
            dma((groups, 2)), dma((groups, 2)),
            root, vec, dma((groups, 2)), dma((groups, 2)),
            pltpu.VMEM((groups, 2, CELLS, states), F32), dma((groups, 2)), dma((groups, 2)),
            vec, vec, vec, vec, vec, vec,
            pltpu.VMEM((groups, count * CELLS, states), F32),
            pltpu.VMEM((cells // 2, SUB, count, 2 * states), F32),
            dma((groups, 2, 2)), dma((groups, 2)),
        ],
        compiler_params=pltpu.CompilerParams(
            collective_id=1, has_side_effects=True, vmem_limit_bytes=VMEM_LIMIT
        ),
    )(
        dna_bases.reshape(bins, BIN_BP),
        stem_weight,
        conv_weight.transpose(0, 2, 1, 3),
        proj_weight,
        emission_head_weight,
        transitions,
    )


def solution(mesh):
    placed = (
        P(("groups", "seq")),
        P(),
        P(None, "cell", None, None),
        P(None, "cell", None),
        P("cell", None, None),
        P("cell", None, None),
    )
    return jax.shard_map(
        per_device,
        mesh=mesh,
        in_specs=placed,
        out_specs=P("cell", ("groups", "seq"), None),
        check_vma=False,
    )
```

```python
import functools

import jax
import jax.numpy as jnp
from jax import lax
from jax.experimental import pallas as pl
from jax.experimental.pallas import tpu as pltpu
from jax.sharding import PartitionSpec as P

BIN_BP = 128
BASE_DILATION = 4
SUB = 8
HALO = 16
MARGIN = 8
WIDTH = 2
CELLS = 8
VMEM_LIMIT = 54800 << 10
MESH = pl.DeviceIdType.MESH
F32 = jnp.float32
BF16 = jnp.bfloat16


def tops(x):
    m = jnp.max(x, axis=-2, keepdims=True)
    return wide_tops(m)


def wide_tops(m):
    half = m.shape[-1] // 2
    shape = m.shape[:-1] + (half,)
    left = jnp.max(m[..., :half], axis=-1, keepdims=True)
    right = jnp.max(m[..., half:], axis=-1, keepdims=True)
    return jnp.concatenate([jnp.broadcast_to(left, shape), jnp.broadcast_to(right, shape)], axis=-1)


def wide_sums(x):
    half = x.shape[-1] // 2
    shape = x.shape[:-1] + (half,)
    left = jnp.sum(x[..., :half], axis=-1, keepdims=True)
    right = jnp.sum(x[..., half:], axis=-1, keepdims=True)
    return jnp.concatenate([jnp.broadcast_to(left, shape), jnp.broadcast_to(right, shape)], axis=-1)


def two_blocks(x):
    half = x.shape[1] // 2
    zero = jnp.zeros((x.shape[0], half), x.dtype)
    return jnp.concatenate(
        [
            jnp.concatenate([x[:, :half], zero], axis=1),
            jnp.concatenate([zero, x[:, half:]], axis=1),
        ],
        axis=0,
    )


def rms(v):
    return v * lax.rsqrt(jnp.mean(v * v, axis=-1, keepdims=True) + 1e-06)


def crf_kernel(
    bases_hbm, stem_hbm, conv_hbm, proj_hbm, head_hbm, trans_hbm, out_ref,
    bases_ref, stem_ref, conv_ref, head_ref, trans_ref, lsem,
    wide_ref, wts_ref, mine0, got0, mine1, got1,
    hs_sem, hr_sem, cs_sem, cr_sem, ws_sem, wr_sem, gs_sem, gr_sem, feat_ref,
    f_ref, trn_ref, off_ref, flip_ref, own_ref, peak_ref, tree_ref, diag_ref,
    root_ref, rown_ref, next_ref, nown_ref, ms_sem, mr_sem,
    twin_ref, town_ref, xs_sem, xr_sem, relays, ls_sem, lr_sem,
    vin, win, vgot, wgot, vout, wout, st_ref, kept_ref, ssem, rsem,
):
    cells, states = head_ref.shape[0], head_ref.shape[2]
    bins = feat_ref.shape[0]
    layers, taps = conv_ref.shape[:2]
    held, padded, wide = conv_hbm.shape[2], conv_ref.shape[2], conv_ref.shape[3]
    count = bins // SUB
    n = lax.axis_size("seq")
    me = lax.axis_index("seq")
    cell = lax.axis_index("cell")
    near = cell + 1 - 2 * (cell % 2)
    far = (cell + 2) % 4
    diag = (near + 2) % 4
    first, second = pl.ds(0, held), pl.ds(held, held)

    pairs = [(bases_hbm, bases_ref)]
    pairs += [(proj_hbm.at[k], wts_ref.at[k, 0, first]) for k in range(layers)]
    pairs += [(conv_hbm.at[k], conv_ref.at[k, :, first]) for k in range(layers)]
    pairs += [(stem_hbm, stem_ref), (trans_hbm, trans_ref), (head_hbm, head_ref)]
    loads = [pltpu.make_async_copy(a, b, lsem.at[i]) for i, (a, b) in enumerate(pairs)]
    for load in loads:
        load.start()
    base_load, proj_loads, conv_loads = loads[0], loads[1 : layers + 1], loads[layers + 1 : -3]
    stem_load, trans_load, head_load = loads[-3:]

    barrier = pltpu.get_barrier_semaphore()
    for peer in (near, far, diag):
        pl.semaphore_signal(barrier, inc=1, device_id={"cell": peer}, device_id_type=MESH)
    for step in (-1, 1):

        @pl.when(jnp.logical_and(me + step >= 0, me + step < n))
        def _():
            pl.semaphore_signal(
                barrier, inc=1, device_id={"seq": me + step, "cell": near}, device_id_type=MESH
            )

    extra = padded - 2 * held
    if extra:
        for layer in range(layers):
            conv_ref[layer, :, pl.ds(2 * held, extra), :] = jnp.zeros((taps, extra, wide), BF16)
            wts_ref[layer, :, pl.ds(2 * held, extra), :] = jnp.zeros((2, extra, wide), BF16)
    base_load.wait()
    inner = jnp.logical_and(me > 0, me < n - 1)
    pl.semaphore_wait(barrier, jnp.where(inner, 5, 4 if n > 1 else 3))

    upward = pltpu.make_async_remote_copy(
        bases_ref.at[pl.ds(bins - HALO, HALO)], wide_ref.at[pl.ds(0, HALO)],
        hs_sem.at[0], hr_sem.at[0],
        device_id={"seq": jnp.minimum(me + 1, n - 1), "cell": near}, device_id_type=MESH,
    )
    downward = pltpu.make_async_remote_copy(
        bases_ref.at[pl.ds(0, HALO)], wide_ref.at[pl.ds(HALO, HALO)],
        hs_sem.at[1], hr_sem.at[1],
        device_id={"seq": jnp.maximum(me - 1, 0), "cell": near}, device_id_type=MESH,
    )

    @pl.when(me < n - 1)
    def _():
        upward.start()

    @pl.when(me > 0)
    def _():
        downward.start()

    def send_conv(layer):
        return pltpu.make_async_remote_copy(
            conv_ref.at[layer, :, first], conv_ref.at[layer, :, second],
            cs_sem.at[layer], cr_sem.at[layer],
            device_id={"cell": near}, device_id_type=MESH,
        )

    def send_weight(layer, k):
        source = wts_ref.at[layer, 1, second] if k == 2 else wts_ref.at[layer, 0, first]
        target = wts_ref.at[layer, 0 if k == 0 else 1, first if k == 2 else second]
        return pltpu.make_async_remote_copy(
            source, target, ws_sem.at[layer, k], wr_sem.at[layer, k],
            device_id={"cell": far if k == 1 else near}, device_id_type=MESH,
        )

    mine, got = (mine0, mine1), (got0, got1)

    def send_hidden(layer):
        return pltpu.make_async_remote_copy(
            mine[layer], got[layer], gs_sem.at[layer], gr_sem.at[layer],
            device_id={"cell": diag}, device_id_type=MESH,
        )

    for layer in range(layers):
        proj_loads[layer].wait()
        if layer == 0:
            send_weight(layer, 1).start()
        conv_loads[layer].wait()
        send_conv(layer).start()
        send_weight(layer, 0).start()

    states_sq = (states, 2 * states)
    eye = lax.broadcasted_iota(jnp.int32, states_sq, 0) == lax.broadcasted_iota(
        jnp.int32, states_sq, 1
    ) % states

    def prepare(p, _):
        raw = jnp.concatenate([trans_ref[2 * p], trans_ref[2 * p + 1]], axis=1)
        peak = jnp.max(raw, axis=0, keepdims=True)
        t = jnp.exp(raw - peak)
        off = jnp.where(eye, 0.0, t)
        peak_ref[p] = peak
        own_ref[p] = jnp.sum(jnp.where(eye, t, 0.0), axis=0, keepdims=True)
        trn_ref[p] = t
        off_ref[p] = off.astype(BF16)
        flip_ref[p] = jnp.concatenate([off[:, :states].T, off[:, states:].T], axis=1).astype(BF16)
        return 0

    trans_load.wait()
    lax.fori_loop(0, cells // 4, prepare, 0)

    columns = lax.broadcasted_iota(jnp.int32, (BIN_BP, 4 * BIN_BP), 1)
    spread = (columns // 4 == lax.broadcasted_iota(jnp.int32, columns.shape, 0)).astype(BF16)
    stem_load.wait()

    @pl.when(me > 0)
    def _():
        upward.wait_recv()

    @pl.when(me == 0)
    def _():
        wide_ref[pl.ds(0, HALO), :] = jnp.zeros((HALO, BIN_BP), jnp.int32)

    @pl.when(me < n - 1)
    def _():
        downward.wait_recv()

    @pl.when(me == n - 1)
    def _():
        wide_ref[pl.ds(HALO, HALO), :] = jnp.zeros((HALO, BIN_BP), jnp.int32)

    bases = jnp.concatenate(
        [wide_ref[pl.ds(0, HALO), :], bases_ref[...], wide_ref[pl.ds(HALO, HALO), :]], axis=0
    )
    repeated = jnp.dot(
        bases.astype(F32).astype(BF16), spread, preferred_element_type=F32
    )
    which = (lax.broadcasted_iota(jnp.int32, repeated.shape, 1) % 4).astype(F32)
    one_hot = jnp.where(repeated == which, 1.0, 0.0).astype(BF16)
    residual = jnp.dot(one_hot, stem_ref[...], preferred_element_type=F32).astype(BF16).astype(F32)
    for layer in range(layers):
        dilation = BASE_DILATION * 2**layer
        rows_in = residual.shape[0]
        place = lax.broadcasted_iota(jnp.int32, residual.shape, 0) + (
            me * bins - (rows_in - bins) // 2
        )
        inside = jnp.logical_and(place >= 0, place < n * bins)
        conv_in = jnp.where(inside, jax.nn.gelu(rms(residual)), 0.0).astype(BF16)
        send_conv(layer).wait_recv()
        tap = [
            lax.dot_general(
                conv_in, conv_ref[layer, k], (((1,), (1,)), ((), ())), preferred_element_type=F32
            )
            for k in range(taps)
        ]
        conv_out = (
            pltpu.roll(tap[0], dilation, 0) + tap[1] + pltpu.roll(tap[2], rows_in - dilation, 0)
        )[MARGIN : rows_in - MARGIN]
        hidden = jax.nn.gelu(conv_out).astype(BF16)
        mine[layer][...] = hidden
        send_hidden(layer).start()
        if layer + 1 < layers:
            send_weight(layer + 1, 1).start()
        send_weight(layer, 1).wait_recv()
        send_weight(layer, 2).start()
        send_weight(layer, 0).wait_recv()
        if layer == 0:
            lax.fori_loop(cells // 4, cells // 2, prepare, 0)
        send_weight(layer, 2).wait_recv()
        send_hidden(layer).wait_recv()
        residual = residual[MARGIN : rows_in - MARGIN] + jnp.dot(
            jnp.concatenate([hidden, got[layer][...]], axis=1),
            wts_ref[layer].reshape(2 * padded, wide),
            preferred_element_type=F32,
        )
    feat_ref[...] = rms(residual).astype(BF16)
    head_load.wait()

    even = me % 2 == 0
    gives = jnp.logical_or(
        jnp.logical_and(even, me >= 2), jnp.logical_and(jnp.logical_not(even), me <= n - 3)
    )
    beside = jnp.minimum(me + 1 - 2 * (me % 2), n - 1)
    groups = cells // 2 // WIDTH

    def send_root(g):
        return [
            pltpu.make_async_remote_copy(
                a.at[g], b.at[g], ms_sem.at[g, i], mr_sem.at[g, i],
                device_id={"seq": beside}, device_id_type=MESH,
            )
            for i, (a, b) in enumerate([(root_ref, next_ref), (rown_ref, nown_ref)])
        ]

    swaps = jnp.logical_and(jnp.logical_or(me == 1, me == n - 2), n > 2)

    def send_near(g):
        return [
            pltpu.make_async_remote_copy(
                a.at[g], b.at[g], xs_sem.at[g, i], xr_sem.at[g, i],
                device_id={"cell": near}, device_id_type=MESH,
            )
            for i, (a, b) in enumerate([(root_ref, twin_ref), (rown_ref, town_ref)])
        ]

    def rates(p, j):
        return jnp.concatenate(
            [f_ref[2 * p + h, pl.ds(j, count, stride=SUB), :] for h in range(2)], axis=1
        )

    def chain(g):
        group = [WIDTH * g + q for q in range(WIDTH)]
        for p in group:
            weight = jnp.concatenate([head_ref[2 * p], head_ref[2 * p + 1]], axis=1)
            e = jnp.dot(feat_ref[...], weight, preferred_element_type=F32) + peak_ref[p]
            f = jnp.exp(e - wide_tops(e))
            f_ref[2 * p] = f[:, :states]
            f_ref[2 * p + 1] = f[:, states:]
        blocks = [two_blocks(off_ref[p]) for p in group]
        xs = [trn_ref[p][None] * rates(p, 0)[:, None, :] for p in group]
        scales = {}
        for j in range(1, SUB):
            for q, p in enumerate(group):
                x = xs[q]
                r = rates(p, j)
                if j == SUB // 2:
                    scales[q] = 1.0 / wide_tops(jnp.max(x, axis=1))
                if j == SUB // 2 + 1:
                    r = r * scales[q]
                h = r * own_ref[p]
                y = jnp.dot(
                    x.astype(BF16).reshape(count * states, 2 * states),
                    blocks[q],
                    preferred_element_type=F32,
                ).reshape(x.shape)
                xs[q] = y * r[:, None, :] + x * h[:, None, :]
        nodes = [[(x[k], None) for k in range(count)] for x in xs]
        place = 0
        width = count
        while width:
            for q in range(WIDTH):
                joined = []
                for k, (x, scale) in enumerate(nodes[q]):
                    slanted = jnp.where(eye, x, 0.0)
                    off = (x - slanted).astype(BF16)
                    own = jnp.sum(slanted, axis=0, keepdims=True)
                    for h in range(2):
                        half = slice(h * states, (h + 1) * states)
                        if width > 1:
                            tree_ref[g, place + k, q, h] = off[:, half]
                            diag_ref[g, place + k, pl.ds(2 * q + h, 1), :] = own[:, half]
                        else:
                            root_ref[g, q, h] = off[:, half]
                            rown_ref[g, pl.ds(2 * q + h, 1), :] = own[:, half]
                    if k % 2 == 0:
                        left, left_scale = x, scale
                    else:
                        y = jnp.dot(
                            left.astype(BF16), two_blocks(off), preferred_element_type=F32
                        )
                        y = y + left * own
                        joined.append(y if scale is None else y * (left_scale * scale))
                nodes[q] = [(y, 1.0 / tops(y)) for y in joined]
            place += width
            width //= 2

        @pl.when(swaps)
        def _():
            for copy in send_near(g):
                copy.start()

        @pl.when(gives)
        def _():
            for copy in send_root(g):
                copy.start()

    rows = lax.broadcasted_iota(jnp.int32, (CELLS, states), 0)

    def through(v, mats, own, back, level=True):
        low = v.astype(BF16)
        out = v * own
        for q in range(WIDTH):
            if back:
                y = lax.dot_general(
                    low, mats[q].reshape(2 * states, states),
                    (((1,), (1,)), ((), ())), preferred_element_type=F32,
                )
            else:
                both = jnp.concatenate([mats[q, 0], mats[q, 1]], axis=1)
                y = jnp.dot(low, both, preferred_element_type=F32)
            out = out + jnp.where(rows == 2 * q, y[:, :states], 0.0)
            out = out + jnp.where(rows == 2 * q + 1, y[:, states:], 0.0)
        return out * (1.0 / jnp.max(v, axis=-1, keepdims=True)) if level else out

    def carry(from_first, starts, arrivals, outs, k, back, g):
        side = -1 if back else 1
        start, arrived, out = starts.at[g], arrivals.at[g], outs.at[g]

        def send(step):
            to = jnp.clip(me + side * step, 0, n - 1)
            return pltpu.make_async_remote_copy(
                out, arrived, ssem.at[g, k, step - 1], rsem.at[g, k],
                device_id={"seq": to, "cell": jnp.where(from_first == 1, near, cell)},
                device_id_type=MESH,
            )

        relayed = relays.at[g, k]
        send_relay = pltpu.make_async_remote_copy(
            out, relayed, ls_sem.at[g, k], lr_sem.at[g, k],
            device_id={"seq": jnp.clip(me + side, 0, n - 1), "cell": near}, device_id_type=MESH,
        )
        odd = from_first % 2 == 1
        hops = jnp.logical_and(odd, from_first >= 3)
        sends = jnp.logical_and(hops, from_first < n - 1)
        turns = jnp.logical_and(from_first == 1, n > 2)
        twice = jnp.logical_and(odd, from_first < n - 2)

        def lead():
            @pl.when(from_first == 0)
            def _():
                start[...] = jnp.ones((CELLS, states), F32)

            @pl.when(jnp.logical_and(from_first == 0, n > 1))
            def _():
                out[...] = through(
                    jnp.ones((CELLS, states), F32), root_ref.at[g], rown_ref[g], back
                )
                if n > 2:
                    send_relay.start()
                send(1).start()

        def run():
            @pl.when(turns)
            def _():
                for copy in send_near(g):
                    copy.wait_recv()
                send_relay.wait_recv()
                out[...] = through(relayed[...], twin_ref.at[g], town_ref[g], back)
                send(2).start()
                send(1).start()

            @pl.when(from_first > 0)
            def _():
                send(1).wait_recv()

            @pl.when(jnp.logical_and(from_first > 0, jnp.logical_not(hops)))
            def _():
                start[...] = arrived[...]

            @pl.when(hops)
            def _():
                for copy in send_root(g):
                    copy.wait_recv()
                start[...] = through(arrived[...], next_ref.at[g], nown_ref[g], back)

            @pl.when(sends)
            def _():
                out[...] = through(start[...], root_ref.at[g], rown_ref[g], back)
                send(1).start()

            @pl.when(jnp.logical_and(twice, hops))
            def _():
                send(2).start()

        def finish():
            @pl.when(jnp.logical_or(jnp.logical_or(sends, turns), jnp.logical_and(from_first == 0, n > 1)))
            def _():
                send(1).wait_send()

            @pl.when(jnp.logical_and(from_first == 0, n > 2))
            def _():
                send_relay.wait_send()

            @pl.when(twice)
            def _():
                send(2).wait_send()

        return lead, run, finish

    def sweep(g, back, last):
        def step_through(v, node):
            return through(v, tree_ref.at[g, node], diag_ref[g, node], back, False)

        edge = count - 1 if back else 0
        chunk = {edge: win[g] if back else vin[g]}
        width = count // 2
        base = 2 * count - 4
        while width >= 1:
            for k in range(0, count, 2 * width):
                if back:
                    end = k + 2 * width - 1
                    chunk[end - width] = step_through(chunk[end], base + end // width)
                else:
                    chunk[k + width] = step_through(chunk[k], base + k // width)
            width //= 2
            if width:
                base -= count // width
        for k in range(count):
            st_ref[g, pl.ds(k * CELLS, CELLS), :] = chunk[k]

        def advance(v, ref, p):
            stacked = jnp.concatenate([v[:, :states], v[:, states:]], axis=0).astype(BF16)
            y = jnp.dot(stacked, ref[p], preferred_element_type=F32)
            y = jnp.concatenate([y[:count, :states], y[count:, states:]], axis=1)
            return y + v * own_ref[p]

        def emit(q, j, v):
            p = WIDTH * g + q
            joint = jnp.log(v) + kept_ref[p, j]
            joint = joint - wide_tops(joint)
            result = jnp.maximum(joint - jnp.log(wide_sums(jnp.exp(joint))), -30.0)
            for h in range(2):
                out_ref[2 * p + h, pl.ds(j, count, stride=SUB), :] = result[
                    :, h * states : (h + 1) * states
                ]

        state = [
            jnp.concatenate(
                [st_ref[g, pl.ds(2 * q + h, count, stride=CELLS), :] for h in range(2)], axis=1
            )
            for q in range(WIDTH)
        ]
        for step in range(SUB):
            j = SUB - 1 - step if back else step
            for q in range(WIDTH):
                p = WIDTH * g + q
                v = state[q]
                if not back or step < SUB - 1:
                    f = rates(p, j)
                    if step % (SUB // 2) == 0:
                        f = f * (1.0 / wide_tops(v))
                    if back:
                        state[q] = advance(v * f, flip_ref, p)
                    else:
                        state[q] = advance(v, off_ref, p) * f
                v = v if back else state[q]
                if last:
                    emit(q, j, v)
                else:
                    kept_ref[p, j] = jnp.log(v)

    rown_ref[...] = jnp.ones_like(rown_ref)
    diag_ref[...] = jnp.ones_like(diag_ref)
    carries = [
        (
            carry(me, vin, vgot, vout, 0, False, g),
            carry(n - 1 - me, win, wgot, wout, 1, True, g),
        )
        for g in range(groups)
    ]
    for g in range(groups):
        chain(g)
        for part in carries[g]:
            part[0]()
    early = 2 * me < n
    late = jnp.logical_not(early)
    for last in (False, True):
        for g in range(groups):
            for k, when in ((0, early), (1, late)):
                way = 1 - k if last else k

                @pl.when(when)
                def _():
                    carries[g][way][1]()
                    sweep(g, way == 1, last)

    for g in range(groups):
        for part in carries[g]:
            part[2]()

    @pl.when(swaps)
    def _():
        for g in range(groups):
            for copy in send_near(g):
                copy.wait_send()

    @pl.when(gives)
    def _():
        for g in range(groups):
            for copy in send_root(g):
                copy.wait_send()

    @pl.when(me < n - 1)
    def _():
        upward.wait_send()

    @pl.when(me > 0)
    def _():
        downward.wait_send()

    for layer in range(layers):
        send_conv(layer).wait_send()
        send_hidden(layer).wait_send()
        for k in range(3):
            send_weight(layer, k).wait_send()


def per_device(dna_bases, stem_weight, conv_weight, proj_weight, emission_head_weight, transitions):
    bins = dna_bases.shape[0] // BIN_BP
    cells, _, states = emission_head_weight.shape
    layers, held, taps, wide = conv_weight.shape
    padded = pl.cdiv(2 * held, 256) * 256
    count = bins // SUB
    groups = cells // 2 // WIDTH
    n = lax.axis_size("seq")
    assert layers == 2 and HALO == layers * MARGIN and MARGIN >= BASE_DILATION * 2 ** (layers - 1)
    assert lax.axis_size("cell") == 4 and 2 * WIDTH <= CELLS and cells % (2 * WIDTH) == 0 and (n == 1 or n % 2 == 0)
    vmem = pl.BlockSpec(memory_space=pltpu.VMEM)
    hbm = pl.BlockSpec(memory_space=pl.ANY)
    vec = pltpu.VMEM((groups, CELLS, states), F32)
    root = pltpu.VMEM((groups, WIDTH, 2, states, states), BF16)
    dma = pltpu.SemaphoreType.DMA
    square = (cells // 2, states, 2 * states)
    row = (cells // 2, 1, 2 * states)
    hidden = [pltpu.VMEM((bins + 2 * (HALO - (k + 1) * MARGIN), padded), BF16) for k in range(layers)]
    return pl.pallas_call(
        crf_kernel,
        name="crf",
        out_shape=jax.ShapeDtypeStruct((cells, bins, states), F32),
        in_specs=[hbm] * 6,
        out_specs=vmem,
        scratch_shapes=[
            pltpu.VMEM((bins, BIN_BP), jnp.int32),
            pltpu.VMEM(stem_weight.shape, BF16),
            pltpu.VMEM((layers, taps, padded, wide), BF16),
            pltpu.VMEM(emission_head_weight.shape, BF16),
            pltpu.VMEM(transitions.shape, F32),
            dma((2 * layers + 4,)),
            pltpu.VMEM((2 * HALO, BIN_BP), jnp.int32),
            pltpu.VMEM((layers, 2, padded, wide), BF16),
            hidden[0], hidden[0], hidden[1], hidden[1],
            dma((2,)), dma((2,)), dma((layers,)), dma((layers,)),
            dma((layers, 3)), dma((layers, 3)), dma((layers,)), dma((layers,)),
            pltpu.VMEM((bins, wide), BF16),
            pltpu.VMEM((cells, bins, states), F32),
            pltpu.VMEM(square, F32),
            pltpu.VMEM(square, BF16),
            pltpu.VMEM(square, BF16),
            pltpu.VMEM(row, F32),
            pltpu.VMEM(row, F32),
            pltpu.VMEM((groups, 2 * count - 2, WIDTH, 2, states, states), BF16),
            pltpu.VMEM((groups, 2 * count - 2, CELLS, states), F32),
            root, vec, root, vec,
            dma((groups, 2)), dma((groups, 2)),
            root, vec, dma((groups, 2)), dma((groups, 2)),
            pltpu.VMEM((groups, 2, CELLS, states), F32), dma((groups, 2)), dma((groups, 2)),
            vec, vec, vec, vec, vec, vec,
            pltpu.VMEM((groups, count * CELLS, states), F32),
            pltpu.VMEM((cells // 2, SUB, count, 2 * states), F32),
            dma((groups, 2, 2)), dma((groups, 2)),
        ],
        compiler_params=pltpu.CompilerParams(
            collective_id=1, has_side_effects=True, vmem_limit_bytes=VMEM_LIMIT
        ),
    )(
        dna_bases.reshape(bins, BIN_BP),
        stem_weight,
        conv_weight.transpose(0, 2, 1, 3),
        proj_weight,
        emission_head_weight,
        transitions,
    )


def solution(mesh):
    placed = (
        P(("groups", "seq")),
        P(),
        P(None, "cell", None, None),
        P(None, "cell", None),
        P("cell", None, None),
        P("cell", None, None),
    )
    return jax.shard_map(
        per_device,
        mesh=mesh,
        in_specs=placed,
        out_specs=P("cell", ("groups", "seq"), None),
        check_vma=False,
    )
```

```python
import functools

import jax
import jax.numpy as jnp
from jax import lax
from jax.experimental import pallas as pl
from jax.experimental.pallas import tpu as pltpu
from jax.sharding import PartitionSpec as P

BIN_BP = 128
BASE_DILATION = 4
SUB = 8
HALO = 16
MARGIN = 8
WIDTH = 2
CELLS = 8
VMEM_LIMIT = 54800 << 10
MESH = pl.DeviceIdType.MESH
F32 = jnp.float32
BF16 = jnp.bfloat16


def tops(x):
    m = jnp.max(x, axis=-2, keepdims=True)
    return wide_tops(m)


def wide_tops(m):
    half = m.shape[-1] // 2
    shape = m.shape[:-1] + (half,)
    left = jnp.max(m[..., :half], axis=-1, keepdims=True)
    right = jnp.max(m[..., half:], axis=-1, keepdims=True)
    return jnp.concatenate([jnp.broadcast_to(left, shape), jnp.broadcast_to(right, shape)], axis=-1)


def wide_sums(x):
    half = x.shape[-1] // 2
    shape = x.shape[:-1] + (half,)
    left = jnp.sum(x[..., :half], axis=-1, keepdims=True)
    right = jnp.sum(x[..., half:], axis=-1, keepdims=True)
    return jnp.concatenate([jnp.broadcast_to(left, shape), jnp.broadcast_to(right, shape)], axis=-1)


def two_blocks(x):
    half = x.shape[1] // 2
    zero = jnp.zeros((x.shape[0], half), x.dtype)
    return jnp.concatenate(
        [
            jnp.concatenate([x[:, :half], zero], axis=1),
            jnp.concatenate([zero, x[:, half:]], axis=1),
        ],
        axis=0,
    )


def rms(v):
    return v * lax.rsqrt(jnp.mean(v * v, axis=-1, keepdims=True) + 1e-06)


def crf_kernel(
    bases_hbm, stem_hbm, conv_hbm, proj_hbm, head_hbm, trans_hbm, out_ref,
    bases_ref, stem_ref, conv_ref, head_ref, trans_ref, lsem,
    wide_ref, wts_ref, mine0, got0, mine1, got1,
    hs_sem, hr_sem, cs_sem, cr_sem, ws_sem, wr_sem, gs_sem, gr_sem, feat_ref,
    f_ref, trn_ref, off_ref, flip_ref, own_ref, peak_ref, tree_ref, diag_ref,
    root_ref, rown_ref, next_ref, nown_ref, ms_sem, mr_sem,
    twin_ref, town_ref, xs_sem, xr_sem, relays, ls_sem, lr_sem,
    vin, win, vgot, wgot, vout, wout, st_ref, kept_ref, ssem, rsem,
):
    cells, states = head_ref.shape[0], head_ref.shape[2]
    bins = feat_ref.shape[0]
    layers, taps = conv_ref.shape[:2]
    held, padded, wide = conv_hbm.shape[2], conv_ref.shape[2], conv_ref.shape[3]
    count = bins // SUB
    n = lax.axis_size("seq")
    me = lax.axis_index("seq")
    cell = lax.axis_index("cell")
    near = cell + 1 - 2 * (cell % 2)
    far = (cell + 2) % 4
    diag = (near + 2) % 4
    first, second = pl.ds(0, held), pl.ds(held, held)

    pairs = [(bases_hbm, bases_ref)]
    pairs += [(proj_hbm.at[k], wts_ref.at[k, 0, first]) for k in range(layers)]
    pairs += [(conv_hbm.at[k], conv_ref.at[k, :, first]) for k in range(layers)]
    pairs += [(stem_hbm, stem_ref), (trans_hbm, trans_ref), (head_hbm, head_ref)]
    loads = [pltpu.make_async_copy(a, b, lsem.at[i]) for i, (a, b) in enumerate(pairs)]
    for load in loads:
        load.start()
    base_load, proj_loads, conv_loads = loads[0], loads[1 : layers + 1], loads[layers + 1 : -3]
    stem_load, trans_load, head_load = loads[-3:]

    barrier = pltpu.get_barrier_semaphore()
    for peer in (near, far, diag):
        pl.semaphore_signal(barrier, inc=1, device_id={"cell": peer}, device_id_type=MESH)
    for step in (-1, 1):

        @pl.when(jnp.logical_and(me + step >= 0, me + step < n))
        def _():
            pl.semaphore_signal(
                barrier, inc=1, device_id={"seq": me + step, "cell": near}, device_id_type=MESH
            )

    rown_ref[...] = jnp.ones_like(rown_ref)
    diag_ref[...] = jnp.ones_like(diag_ref)
    extra = padded - 2 * held
    if extra:
        for layer in range(layers):
            conv_ref[layer, :, pl.ds(2 * held, extra), :] = jnp.zeros((taps, extra, wide), BF16)
            wts_ref[layer, :, pl.ds(2 * held, extra), :] = jnp.zeros((2, extra, wide), BF16)
    base_load.wait()
    inner = jnp.logical_and(me > 0, me < n - 1)
    pl.semaphore_wait(barrier, jnp.where(inner, 5, 4 if n > 1 else 3))

    upward = pltpu.make_async_remote_copy(
        bases_ref.at[pl.ds(bins - HALO, HALO)], wide_ref.at[pl.ds(0, HALO)],
        hs_sem.at[0], hr_sem.at[0],
        device_id={"seq": jnp.minimum(me + 1, n - 1), "cell": near}, device_id_type=MESH,
    )
    downward = pltpu.make_async_remote_copy(
        bases_ref.at[pl.ds(0, HALO)], wide_ref.at[pl.ds(HALO, HALO)],
        hs_sem.at[1], hr_sem.at[1],
        device_id={"seq": jnp.maximum(me - 1, 0), "cell": near}, device_id_type=MESH,
    )

    @pl.when(me < n - 1)
    def _():
        upward.start()

    @pl.when(me > 0)
    def _():
        downward.start()

    def send_conv(layer):
        return pltpu.make_async_remote_copy(
            conv_ref.at[layer, :, first], conv_ref.at[layer, :, second],
            cs_sem.at[layer], cr_sem.at[layer],
            device_id={"cell": near}, device_id_type=MESH,
        )

    def send_weight(layer, k):
        source = wts_ref.at[layer, 1 if k == 2 else 0, first]
        target = wts_ref.at[layer, 0 if k == 0 else 1, first if k == 1 else second]
        return pltpu.make_async_remote_copy(
            source, target, ws_sem.at[layer, k], wr_sem.at[layer, k],
            device_id={"cell": diag if k == 1 else near}, device_id_type=MESH,
        )

    mine, got = (mine0, mine1), (got0, got1)

    def send_hidden(layer):
        return pltpu.make_async_remote_copy(
            mine[layer], got[layer], gs_sem.at[layer], gr_sem.at[layer],
            device_id={"cell": diag}, device_id_type=MESH,
        )

    for layer in range(layers):
        proj_loads[layer].wait()
        if layer == 0:
            send_weight(layer, 1).start()
        conv_loads[layer].wait()
        send_conv(layer).start()
        send_weight(layer, 0).start()

    states_sq = (states, 2 * states)
    eye = lax.broadcasted_iota(jnp.int32, states_sq, 0) == lax.broadcasted_iota(
        jnp.int32, states_sq, 1
    ) % states

    def prepare(p, _):
        raw = jnp.concatenate([trans_ref[2 * p], trans_ref[2 * p + 1]], axis=1)
        peak = jnp.max(raw, axis=0, keepdims=True)
        t = jnp.exp(raw - peak)
        off = jnp.where(eye, 0.0, t)
        peak_ref[p] = peak
        own_ref[p] = jnp.sum(jnp.where(eye, t, 0.0), axis=0, keepdims=True)
        trn_ref[p] = t
        off_ref[p] = off.astype(BF16)
        flip_ref[p] = jnp.concatenate([off[:, :states].T, off[:, states:].T], axis=1).astype(BF16)
        return 0

    trans_load.wait()
    lax.fori_loop(0, cells // 4, prepare, 0)

    columns = lax.broadcasted_iota(jnp.int32, (BIN_BP, 4 * BIN_BP), 1)
    spread = (columns // 4 == lax.broadcasted_iota(jnp.int32, columns.shape, 0)).astype(BF16)
    stem_load.wait()

    @pl.when(me > 0)
    def _():
        upward.wait_recv()

    @pl.when(me == 0)
    def _():
        wide_ref[pl.ds(0, HALO), :] = jnp.zeros((HALO, BIN_BP), jnp.int32)

    @pl.when(me < n - 1)
    def _():
        downward.wait_recv()

    @pl.when(me == n - 1)
    def _():
        wide_ref[pl.ds(HALO, HALO), :] = jnp.zeros((HALO, BIN_BP), jnp.int32)

    bases = jnp.concatenate(
        [wide_ref[pl.ds(0, HALO), :], bases_ref[...], wide_ref[pl.ds(HALO, HALO), :]], axis=0
    )
    repeated = jnp.dot(
        bases.astype(F32).astype(BF16), spread, preferred_element_type=F32
    )
    which = (lax.broadcasted_iota(jnp.int32, repeated.shape, 1) % 4).astype(F32)
    one_hot = jnp.where(repeated == which, 1.0, 0.0).astype(BF16)
    residual = jnp.dot(one_hot, stem_ref[...], preferred_element_type=F32).astype(BF16).astype(F32)
    for layer in range(layers):
        dilation = BASE_DILATION * 2**layer
        rows_in = residual.shape[0]
        place = lax.broadcasted_iota(jnp.int32, residual.shape, 0) + (
            me * bins - (rows_in - bins) // 2
        )
        inside = jnp.logical_and(place >= 0, place < n * bins)
        conv_in = jnp.where(inside, jax.nn.gelu(rms(residual)), 0.0).astype(BF16)
        send_conv(layer).wait_recv()
        tap = [
            lax.dot_general(
                conv_in, conv_ref[layer, k], (((1,), (1,)), ((), ())), preferred_element_type=F32
            )
            for k in range(taps)
        ]
        conv_out = (
            pltpu.roll(tap[0], dilation, 0) + tap[1] + pltpu.roll(tap[2], rows_in - dilation, 0)
        )[MARGIN : rows_in - MARGIN]
        hidden = jax.nn.gelu(conv_out).astype(BF16)
        mine[layer][...] = hidden
        send_hidden(layer).start()
        if layer + 1 < layers:
            send_weight(layer + 1, 1).start()
        send_weight(layer, 1).wait_recv()
        send_weight(layer, 2).start()
        send_weight(layer, 0).wait_recv()
        if layer == 0:
            lax.fori_loop(cells // 4, cells // 2, prepare, 0)
        send_weight(layer, 2).wait_recv()
        send_hidden(layer).wait_recv()
        residual = residual[MARGIN : rows_in - MARGIN] + jnp.dot(
            jnp.concatenate([hidden, got[layer][...]], axis=1),
            wts_ref[layer].reshape(2 * padded, wide),
            preferred_element_type=F32,
        )
    feat_ref[...] = rms(residual).astype(BF16)
    head_load.wait()

    even = me % 2 == 0
    gives = jnp.logical_or(
        jnp.logical_and(even, me >= 2), jnp.logical_and(jnp.logical_not(even), me <= n - 3)
    )
    beside = jnp.minimum(me + 1 - 2 * (me % 2), n - 1)
    groups = cells // 2 // WIDTH

    def send_root(g):
        return [
            pltpu.make_async_remote_copy(
                a.at[g], b.at[g], ms_sem.at[g, i], mr_sem.at[g, i],
                device_id={"seq": beside}, device_id_type=MESH,
            )
            for i, (a, b) in enumerate([(root_ref, next_ref), (rown_ref, nown_ref)])
        ]

    swaps = jnp.logical_and(jnp.logical_or(me == 1, me == n - 2), n > 2)

    def send_near(g):
        return [
            pltpu.make_async_remote_copy(
                a.at[g], b.at[g], xs_sem.at[g, i], xr_sem.at[g, i],
                device_id={"cell": near}, device_id_type=MESH,
            )
            for i, (a, b) in enumerate([(root_ref, twin_ref), (rown_ref, town_ref)])
        ]

    def rates(p, j):
        return jnp.concatenate(
            [f_ref[2 * p + h, pl.ds(j, count, stride=SUB), :] for h in range(2)], axis=1
        )

    def chain(g):
        group = [WIDTH * g + q for q in range(WIDTH)]
        for p in group:
            weight = jnp.concatenate([head_ref[2 * p], head_ref[2 * p + 1]], axis=1)
            e = jnp.dot(feat_ref[...], weight, preferred_element_type=F32) + peak_ref[p]
            f = jnp.exp(e - wide_tops(e))
            f_ref[2 * p] = f[:, :states]
            f_ref[2 * p + 1] = f[:, states:]
        blocks = [two_blocks(off_ref[p]) for p in group]
        xs = [trn_ref[p][None] * rates(p, 0)[:, None, :] for p in group]
        scales = {}
        for j in range(1, SUB):
            for q, p in enumerate(group):
                x = xs[q]
                r = rates(p, j)
                if j == SUB // 2:
                    scales[q] = 1.0 / wide_tops(jnp.max(x, axis=1))
                if j == SUB // 2 + 1:
                    r = r * scales[q]
                h = r * own_ref[p]
                y = jnp.dot(
                    x.astype(BF16).reshape(count * states, 2 * states),
                    blocks[q],
                    preferred_element_type=F32,
                ).reshape(x.shape)
                xs[q] = y * r[:, None, :] + x * h[:, None, :]
        nodes = [[(x[k], None) for k in range(count)] for x in xs]

        def parted(x):
            slanted = jnp.where(eye, x, 0.0)
            return (x - slanted).astype(BF16), jnp.sum(slanted, axis=0, keepdims=True)

        def joined(left, off, own):
            y = jnp.dot(left.astype(BF16), two_blocks(off), preferred_element_type=F32)
            return y + left * own

        place = 0
        width = count
        while width > 1:
            following = [[] for _ in range(WIDTH)]
            ends = []
            for q in range(WIDTH):
                for k, (x, scale) in enumerate(nodes[q]):
                    off, own = parted(x)
                    for h in range(2):
                        half = slice(h * states, (h + 1) * states)
                        tree_ref[g, place + k, q, h] = off[:, half]
                        diag_ref[g, place + k, pl.ds(2 * q + h, 1), :] = own[:, half]
                    if k % 2 == 0:
                        left, left_scale = x, scale
                    elif width == 2:
                        ends.append((left, off, own))
                    else:
                        y = joined(left, off, own)
                        y = y if scale is None else y * (left_scale * scale)
                        following[q].append((y, 1.0 / tops(y) if width == count else None))
            nodes = following
            place += width
            width //= 2

        @pl.when(jnp.logical_and(me > 0, me < n - 1))
        def _():
            for q in range(WIDTH):
                off, own = parted(joined(*ends[q]))
                for h in range(2):
                    half = slice(h * states, (h + 1) * states)
                    root_ref[g, q, h] = off[:, half]
                    rown_ref[g, pl.ds(2 * q + h, 1), :] = own[:, half]

        @pl.when(swaps)
        def _():
            for copy in send_near(g):
                copy.start()

        @pl.when(gives)
        def _():
            for copy in send_root(g):
                copy.start()

    rows = lax.broadcasted_iota(jnp.int32, (CELLS, states), 0)

    def through(v, mats, own, back, level=True):
        low = v.astype(BF16)
        out = v * own
        for q in range(WIDTH):
            if back:
                y = lax.dot_general(
                    low, mats[q].reshape(2 * states, states),
                    (((1,), (1,)), ((), ())), preferred_element_type=F32,
                )
            else:
                both = jnp.concatenate([mats[q, 0], mats[q, 1]], axis=1)
                y = jnp.dot(low, both, preferred_element_type=F32)
            out = out + jnp.where(rows == 2 * q, y[:, :states], 0.0)
            out = out + jnp.where(rows == 2 * q + 1, y[:, states:], 0.0)
        return out * (1.0 / jnp.max(v, axis=-1, keepdims=True)) if level else out

    def carry(from_first, starts, arrivals, outs, k, back, g):
        side = -1 if back else 1
        start, arrived, out = starts.at[g], arrivals.at[g], outs.at[g]

        def send(step):
            to = jnp.clip(me + side * step, 0, n - 1)
            return pltpu.make_async_remote_copy(
                out, arrived, ssem.at[g, k, step - 1], rsem.at[g, k],
                device_id={"seq": to, "cell": jnp.where(from_first == 1, near, cell)},
                device_id_type=MESH,
            )

        relayed = relays.at[g, k]
        send_relay = pltpu.make_async_remote_copy(
            out, relayed, ls_sem.at[g, k], lr_sem.at[g, k],
            device_id={"seq": jnp.clip(me + side, 0, n - 1), "cell": near}, device_id_type=MESH,
        )
        odd = from_first % 2 == 1
        hops = jnp.logical_and(odd, from_first >= 3)
        sends = jnp.logical_and(hops, from_first < n - 1)
        turns = jnp.logical_and(from_first == 1, n > 2)
        twice = jnp.logical_and(odd, from_first < n - 2)

        def lead():
            @pl.when(from_first == 0)
            def _():
                start[...] = jnp.ones((CELLS, states), F32)

            @pl.when(jnp.logical_and(from_first == 0, n > 1))
            def _():
                v = jnp.ones((CELLS, states), F32)
                for node in (2 * count - 3, 2 * count - 4) if back else (2 * count - 4, 2 * count - 3):
                    v = through(v, tree_ref.at[g, node], diag_ref[g, node], back)
                out[...] = v
                if n > 2:
                    send_relay.start()
                send(1).start()

        def run():
            @pl.when(turns)
            def _():
                for copy in send_near(g):
                    copy.wait_recv()
                send_relay.wait_recv()
                out[...] = through(relayed[...], twin_ref.at[g], town_ref[g], back)
                send(2).start()
                send(1).start()

            @pl.when(from_first > 0)
            def _():
                send(1).wait_recv()

            @pl.when(jnp.logical_and(from_first > 0, jnp.logical_not(hops)))
            def _():
                start[...] = arrived[...]

            @pl.when(hops)
            def _():
                for copy in send_root(g):
                    copy.wait_recv()
                start[...] = through(arrived[...], next_ref.at[g], nown_ref[g], back)

            @pl.when(sends)
            def _():
                out[...] = through(start[...], root_ref.at[g], rown_ref[g], back)
                send(1).start()

            @pl.when(jnp.logical_and(twice, hops))
            def _():
                send(2).start()

        def finish():
            @pl.when(jnp.logical_or(jnp.logical_or(sends, turns), jnp.logical_and(from_first == 0, n > 1)))
            def _():
                send(1).wait_send()

            @pl.when(jnp.logical_and(from_first == 0, n > 2))
            def _():
                send_relay.wait_send()

            @pl.when(twice)
            def _():
                send(2).wait_send()

        return lead, run, finish

    def sweep(g, back, last):
        def step_through(v, node):
            return through(v, tree_ref.at[g, node], diag_ref[g, node], back, False)

        edge = count - 1 if back else 0
        chunk = {edge: win[g] if back else vin[g]}
        width = count // 2
        base = 2 * count - 4
        while width >= 1:
            for k in range(0, count, 2 * width):
                if back:
                    end = k + 2 * width - 1
                    chunk[end - width] = step_through(chunk[end], base + end // width)
                else:
                    chunk[k + width] = step_through(chunk[k], base + k // width)
            width //= 2
            if width:
                base -= count // width
        for k in range(count):
            st_ref[g, pl.ds(k * CELLS, CELLS), :] = chunk[k]

        def advance(v, ref, p):
            stacked = jnp.concatenate([v[:, :states], v[:, states:]], axis=0).astype(BF16)
            y = jnp.dot(stacked, ref[p], preferred_element_type=F32)
            y = jnp.concatenate([y[:count, :states], y[count:, states:]], axis=1)
            return y + v * own_ref[p]

        def emit(q, j, v):
            p = WIDTH * g + q
            joint = jnp.log(v) + kept_ref[p, j]
            joint = joint - wide_tops(joint)
            result = jnp.maximum(joint - jnp.log(wide_sums(jnp.exp(joint))), -30.0)
            for h in range(2):
                out_ref[2 * p + h, pl.ds(j, count, stride=SUB), :] = result[
                    :, h * states : (h + 1) * states
                ]

        state = [
            jnp.concatenate(
                [st_ref[g, pl.ds(2 * q + h, count, stride=CELLS), :] for h in range(2)], axis=1
            )
            for q in range(WIDTH)
        ]
        for step in range(SUB):
            j = SUB - 1 - step if back else step
            for q in range(WIDTH):
                p = WIDTH * g + q
                v = state[q]
                if not back or step < SUB - 1:
                    f = rates(p, j)
                    if step % (SUB // 2) == 0:
                        f = f * (1.0 / wide_tops(v))
                    if back:
                        state[q] = advance(v * f, flip_ref, p)
                    else:
                        state[q] = advance(v, off_ref, p) * f
                v = v if back else state[q]
                if last:
                    emit(q, j, v)
                else:
                    kept_ref[p, j] = jnp.log(v)

    carries = [
        (
            carry(me, vin, vgot, vout, 0, False, g),
            carry(n - 1 - me, win, wgot, wout, 1, True, g),
        )
        for g in range(groups)
    ]
    for g in range(groups):
        chain(g)
        for part in carries[g]:
            part[0]()
    early = 2 * me < n
    late = jnp.logical_not(early)
    for last in (False, True):
        for g in range(groups):
            for k, when in ((0, early), (1, late)):
                way = 1 - k if last else k

                @pl.when(when)
                def _():
                    carries[g][way][1]()
                    sweep(g, way == 1, last)

    for g in range(groups):
        for part in carries[g]:
            part[2]()

    @pl.when(swaps)
    def _():
        for g in range(groups):
            for copy in send_near(g):
                copy.wait_send()

    @pl.when(gives)
    def _():
        for g in range(groups):
            for copy in send_root(g):
                copy.wait_send()

    @pl.when(me < n - 1)
    def _():
        upward.wait_send()

    @pl.when(me > 0)
    def _():
        downward.wait_send()

    for layer in range(layers):
        send_conv(layer).wait_send()
        send_hidden(layer).wait_send()
        for k in range(3):
            send_weight(layer, k).wait_send()


def per_device(dna_bases, stem_weight, conv_weight, proj_weight, emission_head_weight, transitions):
    bins = dna_bases.shape[0] // BIN_BP
    cells, _, states = emission_head_weight.shape
    layers, held, taps, wide = conv_weight.shape
    padded = pl.cdiv(2 * held, 256) * 256
    count = bins // SUB
    groups = cells // 2 // WIDTH
    n = lax.axis_size("seq")
    assert layers == 2 and HALO == layers * MARGIN and MARGIN >= BASE_DILATION * 2 ** (layers - 1)
    assert lax.axis_size("cell") == 4 and 2 * WIDTH <= CELLS and cells % (2 * WIDTH) == 0 and (n == 1 or n % 2 == 0)
    vmem = pl.BlockSpec(memory_space=pltpu.VMEM)
    hbm = pl.BlockSpec(memory_space=pl.ANY)
    vec = pltpu.VMEM((groups, CELLS, states), F32)
    root = pltpu.VMEM((groups, WIDTH, 2, states, states), BF16)
    dma = pltpu.SemaphoreType.DMA
    square = (cells // 2, states, 2 * states)
    row = (cells // 2, 1, 2 * states)
    hidden = [pltpu.VMEM((bins + 2 * (HALO - (k + 1) * MARGIN), padded), BF16) for k in range(layers)]
    return pl.pallas_call(
        crf_kernel,
        name="crf",
        out_shape=jax.ShapeDtypeStruct((cells, bins, states), F32),
        in_specs=[hbm] * 6,
        out_specs=vmem,
        scratch_shapes=[
            pltpu.VMEM((bins, BIN_BP), jnp.int32),
            pltpu.VMEM(stem_weight.shape, BF16),
            pltpu.VMEM((layers, taps, padded, wide), BF16),
            pltpu.VMEM(emission_head_weight.shape, BF16),
            pltpu.VMEM(transitions.shape, F32),
            dma((2 * layers + 4,)),
            pltpu.VMEM((2 * HALO, BIN_BP), jnp.int32),
            pltpu.VMEM((layers, 2, padded, wide), BF16),
            hidden[0], hidden[0], hidden[1], hidden[1],
            dma((2,)), dma((2,)), dma((layers,)), dma((layers,)),
            dma((layers, 3)), dma((layers, 3)), dma((layers,)), dma((layers,)),
            pltpu.VMEM((bins, wide), BF16),
            pltpu.VMEM((cells, bins, states), F32),
            pltpu.VMEM(square, F32),
            pltpu.VMEM(square, BF16),
            pltpu.VMEM(square, BF16),
            pltpu.VMEM(row, F32),
            pltpu.VMEM(row, F32),
            pltpu.VMEM((groups, 2 * count - 2, WIDTH, 2, states, states), BF16),
            pltpu.VMEM((groups, 2 * count - 2, CELLS, states), F32),
            root, vec, root, vec,
            dma((groups, 2)), dma((groups, 2)),
            root, vec, dma((groups, 2)), dma((groups, 2)),
            pltpu.VMEM((groups, 2, CELLS, states), F32), dma((groups, 2)), dma((groups, 2)),
            vec, vec, vec, vec, vec, vec,
            pltpu.VMEM((groups, count * CELLS, states), F32),
            pltpu.VMEM((cells // 2, SUB, count, 2 * states), F32),
            dma((groups, 2, 2)), dma((groups, 2)),
        ],
        compiler_params=pltpu.CompilerParams(
            collective_id=1, has_side_effects=True, vmem_limit_bytes=VMEM_LIMIT
        ),
    )(
        dna_bases.reshape(bins, BIN_BP),
        stem_weight,
        conv_weight.transpose(0, 2, 1, 3),
        proj_weight,
        emission_head_weight,
        transitions,
    )


def solution(mesh):
    placed = (
        P(("groups", "seq")),
        P(),
        P(None, "cell", None, None),
        P(None, "cell", None),
        P("cell", None, None),
        P("cell", None, None),
    )
    return jax.shard_map(
        per_device,
        mesh=mesh,
        in_specs=placed,
        out_specs=P("cell", ("groups", "seq"), None),
        check_vma=False,
    )
```

```python
import functools

import jax
import jax.numpy as jnp
from jax import lax
from jax.experimental import pallas as pl
from jax.experimental.pallas import tpu as pltpu
from jax.sharding import PartitionSpec as P

BIN_BP = 128
BASE_DILATION = 4
SUB = 8
HALO = 16
MARGIN = 8
WIDTH = 2
CELLS = 8
VMEM_LIMIT = 54800 << 10
MESH = pl.DeviceIdType.MESH
F32 = jnp.float32
BF16 = jnp.bfloat16


def tops(x):
    m = jnp.max(x, axis=-2, keepdims=True)
    return wide_tops(m)


def wide_tops(m):
    half = m.shape[-1] // 2
    shape = m.shape[:-1] + (half,)
    left = jnp.max(m[..., :half], axis=-1, keepdims=True)
    right = jnp.max(m[..., half:], axis=-1, keepdims=True)
    return jnp.concatenate([jnp.broadcast_to(left, shape), jnp.broadcast_to(right, shape)], axis=-1)


def wide_sums(x):
    half = x.shape[-1] // 2
    shape = x.shape[:-1] + (half,)
    left = jnp.sum(x[..., :half], axis=-1, keepdims=True)
    right = jnp.sum(x[..., half:], axis=-1, keepdims=True)
    return jnp.concatenate([jnp.broadcast_to(left, shape), jnp.broadcast_to(right, shape)], axis=-1)


def two_blocks(x):
    half = x.shape[1] // 2
    zero = jnp.zeros((x.shape[0], half), x.dtype)
    return jnp.concatenate(
        [
            jnp.concatenate([x[:, :half], zero], axis=1),
            jnp.concatenate([zero, x[:, half:]], axis=1),
        ],
        axis=0,
    )


def rms(v):
    return v * lax.rsqrt(jnp.mean(v * v, axis=-1, keepdims=True) + 1e-06)


def crf_kernel(
    bases_hbm, stem_hbm, conv_hbm, proj_hbm, head_hbm, trans_hbm, out_ref,
    bases_ref, stem_ref, conv_ref, head_ref, trans_ref, lsem,
    wide_ref, wts_ref, mine0, got0, mine1, got1,
    hs_sem, hr_sem, cs_sem, cr_sem, ws_sem, wr_sem, gs_sem, gr_sem, feat_ref,
    f_ref, trn_ref, off_ref, flip_ref, own_ref, peak_ref, tree_ref, diag_ref,
    root_ref, rown_ref, next_ref, nown_ref, ms_sem, mr_sem,
    twin_ref, town_ref, xs_sem, xr_sem, relays, ls_sem, lr_sem,
    vin, win, vgot, wgot, vout, wout, st_ref, kept_ref, ssem, rsem,
):
    cells, states = head_ref.shape[0], head_ref.shape[2]
    bins = feat_ref.shape[0]
    layers, taps = conv_ref.shape[:2]
    held, padded, wide = conv_hbm.shape[2], conv_ref.shape[2], conv_ref.shape[3]
    count = bins // SUB
    n = lax.axis_size("seq")
    me = lax.axis_index("seq")
    cell = lax.axis_index("cell")
    near = cell + 1 - 2 * (cell % 2)
    far = (cell + 2) % 4
    diag = (near + 2) % 4
    first, second = pl.ds(0, held), pl.ds(held, held)

    pairs = [(bases_hbm, bases_ref)]
    pairs += [(proj_hbm.at[k], wts_ref.at[k, 0, first]) for k in range(layers)]
    pairs += [(conv_hbm.at[k], conv_ref.at[k, :, first]) for k in range(layers)]
    pairs += [(stem_hbm, stem_ref), (trans_hbm, trans_ref), (head_hbm, head_ref)]
    loads = [pltpu.make_async_copy(a, b, lsem.at[i]) for i, (a, b) in enumerate(pairs)]
    for load in loads:
        load.start()
    base_load, proj_loads, conv_loads = loads[0], loads[1 : layers + 1], loads[layers + 1 : -3]
    stem_load, trans_load, head_load = loads[-3:]

    barrier = pltpu.get_barrier_semaphore()
    for peer in (near, far, diag):
        pl.semaphore_signal(barrier, inc=1, device_id={"cell": peer}, device_id_type=MESH)
    for step in (-1, 1):

        @pl.when(jnp.logical_and(me + step >= 0, me + step < n))
        def _():
            pl.semaphore_signal(
                barrier, inc=1, device_id={"seq": me + step, "cell": near}, device_id_type=MESH
            )

    rown_ref[...] = jnp.ones_like(rown_ref)
    diag_ref[...] = jnp.ones_like(diag_ref)
    extra = padded - 2 * held
    if extra:
        for layer in range(layers):
            conv_ref[layer, :, pl.ds(2 * held, extra), :] = jnp.zeros((taps, extra, wide), BF16)
            wts_ref[layer, :, pl.ds(2 * held, extra), :] = jnp.zeros((2, extra, wide), BF16)
    base_load.wait()
    inner = jnp.logical_and(me > 0, me < n - 1)
    pl.semaphore_wait(barrier, jnp.where(inner, 5, 4 if n > 1 else 3))

    upward = pltpu.make_async_remote_copy(
        bases_ref.at[pl.ds(bins - HALO, HALO)], wide_ref.at[pl.ds(0, HALO)],
        hs_sem.at[0], hr_sem.at[0],
        device_id={"seq": jnp.minimum(me + 1, n - 1), "cell": near}, device_id_type=MESH,
    )
    downward = pltpu.make_async_remote_copy(
        bases_ref.at[pl.ds(0, HALO)], wide_ref.at[pl.ds(HALO, HALO)],
        hs_sem.at[1], hr_sem.at[1],
        device_id={"seq": jnp.maximum(me - 1, 0), "cell": near}, device_id_type=MESH,
    )

    @pl.when(me < n - 1)
    def _():
        upward.start()

    @pl.when(me > 0)
    def _():
        downward.start()

    def send_conv(layer):
        return pltpu.make_async_remote_copy(
            conv_ref.at[layer, :, first], conv_ref.at[layer, :, second],
            cs_sem.at[layer], cr_sem.at[layer],
            device_id={"cell": near}, device_id_type=MESH,
        )

    def send_weight(layer, k):
        source = wts_ref.at[layer, 1 if k == 2 else 0, first]
        target = wts_ref.at[layer, 0 if k == 0 else 1, first if k == 1 else second]
        return pltpu.make_async_remote_copy(
            source, target, ws_sem.at[layer, k], wr_sem.at[layer, k],
            device_id={"cell": diag if k == 1 else near}, device_id_type=MESH,
        )

    mine, got = (mine0, mine1), (got0, got1)

    def send_hidden(layer):
        return pltpu.make_async_remote_copy(
            mine[layer], got[layer], gs_sem.at[layer], gr_sem.at[layer],
            device_id={"cell": diag}, device_id_type=MESH,
        )

    for layer in range(layers):
        proj_loads[layer].wait()
        if layer == 0:
            send_weight(layer, 1).start()
        conv_loads[layer].wait()
        send_conv(layer).start()
        send_weight(layer, 0).start()

    states_sq = (states, 2 * states)
    eye = lax.broadcasted_iota(jnp.int32, states_sq, 0) == lax.broadcasted_iota(
        jnp.int32, states_sq, 1
    ) % states

    def prepare(p, _):
        raw = jnp.concatenate([trans_ref[2 * p], trans_ref[2 * p + 1]], axis=1)
        peak = jnp.max(raw, axis=0, keepdims=True)
        t = jnp.exp(raw - peak)
        off = jnp.where(eye, 0.0, t)
        peak_ref[p] = peak
        own_ref[p] = jnp.sum(jnp.where(eye, t, 0.0), axis=0, keepdims=True)
        trn_ref[p] = t
        off_ref[p] = off.astype(BF16)
        flip_ref[p] = jnp.concatenate([off[:, :states].T, off[:, states:].T], axis=1).astype(BF16)
        return 0

    trans_load.wait()
    lax.fori_loop(0, cells // 4, prepare, 0)

    columns = lax.broadcasted_iota(jnp.int32, (BIN_BP, 4 * BIN_BP), 1)
    spread = (columns // 4 == lax.broadcasted_iota(jnp.int32, columns.shape, 0)).astype(BF16)
    stem_load.wait()

    @pl.when(me > 0)
    def _():
        upward.wait_recv()

    @pl.when(me == 0)
    def _():
        wide_ref[pl.ds(0, HALO), :] = jnp.zeros((HALO, BIN_BP), jnp.int32)

    @pl.when(me < n - 1)
    def _():
        downward.wait_recv()

    @pl.when(me == n - 1)
    def _():
        wide_ref[pl.ds(HALO, HALO), :] = jnp.zeros((HALO, BIN_BP), jnp.int32)

    bases = jnp.concatenate(
        [wide_ref[pl.ds(0, HALO), :], bases_ref[...], wide_ref[pl.ds(HALO, HALO), :]], axis=0
    )
    repeated = jnp.dot(
        bases.astype(F32).astype(BF16), spread, preferred_element_type=F32
    )
    which = (lax.broadcasted_iota(jnp.int32, repeated.shape, 1) % 4).astype(F32)
    one_hot = jnp.where(repeated == which, 1.0, 0.0).astype(BF16)
    residual = jnp.dot(one_hot, stem_ref[...], preferred_element_type=F32).astype(BF16).astype(F32)
    for layer in range(layers):
        dilation = BASE_DILATION * 2**layer
        rows_in = residual.shape[0]
        place = lax.broadcasted_iota(jnp.int32, residual.shape, 0) + (
            me * bins - (rows_in - bins) // 2
        )
        inside = jnp.logical_and(place >= 0, place < n * bins)
        conv_in = jnp.where(inside, jax.nn.gelu(rms(residual)), 0.0).astype(BF16)
        send_conv(layer).wait_recv()
        tap = [
            lax.dot_general(
                conv_in, conv_ref[layer, k], (((1,), (1,)), ((), ())), preferred_element_type=F32
            )
            for k in range(taps)
        ]
        conv_out = (
            pltpu.roll(tap[0], dilation, 0) + tap[1] + pltpu.roll(tap[2], rows_in - dilation, 0)
        )[MARGIN : rows_in - MARGIN]
        hidden = jax.nn.gelu(conv_out).astype(BF16)
        mine[layer][...] = hidden
        send_hidden(layer).start()
        if layer + 1 < layers:
            send_weight(layer + 1, 1).start()
        send_weight(layer, 1).wait_recv()
        send_weight(layer, 2).start()
        send_weight(layer, 0).wait_recv()
        if layer == 0:
            lax.fori_loop(cells // 4, cells // 2, prepare, 0)
        send_weight(layer, 2).wait_recv()
        send_hidden(layer).wait_recv()
        residual = residual[MARGIN : rows_in - MARGIN] + jnp.dot(
            jnp.concatenate([hidden, got[layer][...]], axis=1),
            wts_ref[layer].reshape(2 * padded, wide),
            preferred_element_type=F32,
        )
    feat_ref[...] = rms(residual).astype(BF16)
    head_load.wait()

    even = me % 2 == 0
    gives = jnp.logical_or(
        jnp.logical_and(even, me >= 2), jnp.logical_and(jnp.logical_not(even), me <= n - 3)
    )
    beside = jnp.minimum(me + 1 - 2 * (me % 2), n - 1)
    groups = cells // 2 // WIDTH

    def send_root(g):
        return [
            pltpu.make_async_remote_copy(
                a.at[g], b.at[g], ms_sem.at[g, i], mr_sem.at[g, i],
                device_id={"seq": beside}, device_id_type=MESH,
            )
            for i, (a, b) in enumerate([(root_ref, next_ref), (rown_ref, nown_ref)])
        ]

    swaps = jnp.logical_and(jnp.logical_or(me == 1, me == n - 2), n > 2)

    def send_near(g):
        return [
            pltpu.make_async_remote_copy(
                a.at[g], b.at[g], xs_sem.at[g, i], xr_sem.at[g, i],
                device_id={"cell": near}, device_id_type=MESH,
            )
            for i, (a, b) in enumerate([(root_ref, twin_ref), (rown_ref, town_ref)])
        ]

    def rates(p, j):
        return jnp.concatenate(
            [f_ref[2 * p + h, pl.ds(j, count, stride=SUB), :] for h in range(2)], axis=1
        )

    def chain(g):
        group = [WIDTH * g + q for q in range(WIDTH)]
        for p in group:
            weight = jnp.concatenate([head_ref[2 * p], head_ref[2 * p + 1]], axis=1)
            e = jnp.dot(feat_ref[...], weight, preferred_element_type=F32) + peak_ref[p]
            f = jnp.exp(e - wide_tops(e))
            f_ref[2 * p] = f[:, :states]
            f_ref[2 * p + 1] = f[:, states:]
        blocks = [two_blocks(off_ref[p]) for p in group]
        xs = [trn_ref[p][None] * rates(p, 0)[:, None, :] for p in group]
        for j in range(1, SUB):
            for q, p in enumerate(group):
                x = xs[q]
                r = rates(p, j)
                h = r * own_ref[p]
                y = jnp.dot(
                    x.astype(BF16).reshape(count * states, 2 * states),
                    blocks[q],
                    preferred_element_type=F32,
                ).reshape(x.shape)
                xs[q] = y * r[:, None, :] + x * h[:, None, :]
        nodes = [[(x[k], 1.0 / tops(x[k])) for k in range(count)] for x in xs]

        def parted(x):
            slanted = jnp.where(eye, x, 0.0)
            return (x - slanted).astype(BF16), jnp.sum(slanted, axis=0, keepdims=True)

        def joined(left, off, own):
            y = jnp.dot(left.astype(BF16), two_blocks(off), preferred_element_type=F32)
            return y + left * own

        place = 0
        width = count
        while width > 1:
            following = [[] for _ in range(WIDTH)]
            ends = []
            for q in range(WIDTH):
                for k, (x, scale) in enumerate(nodes[q]):
                    off, own = parted(x)
                    for h in range(2):
                        half = slice(h * states, (h + 1) * states)
                        tree_ref[g, place + k, q, h] = off[:, half]
                        diag_ref[g, place + k, pl.ds(2 * q + h, 1), :] = own[:, half]
                    if k % 2 == 0:
                        left, left_scale = x, scale
                    elif width == 2:
                        ends.append((left, off, own))
                    else:
                        y = joined(left, off, own)
                        y = y if scale is None else y * (left_scale * scale)
                        following[q].append((y, None))
            nodes = following
            place += width
            width //= 2

        @pl.when(jnp.logical_and(me > 0, me < n - 1))
        def _():
            for q in range(WIDTH):
                off, own = parted(joined(*ends[q]))
                for h in range(2):
                    half = slice(h * states, (h + 1) * states)
                    root_ref[g, q, h] = off[:, half]
                    rown_ref[g, pl.ds(2 * q + h, 1), :] = own[:, half]

        @pl.when(swaps)
        def _():
            for copy in send_near(g):
                copy.start()

        @pl.when(gives)
        def _():
            for copy in send_root(g):
                copy.start()

    rows = lax.broadcasted_iota(jnp.int32, (CELLS, states), 0)

    def through(v, mats, own, back, level=True):
        low = v.astype(BF16)
        out = v * own
        for q in range(WIDTH):
            if back:
                y = lax.dot_general(
                    low, mats[q].reshape(2 * states, states),
                    (((1,), (1,)), ((), ())), preferred_element_type=F32,
                )
            else:
                both = jnp.concatenate([mats[q, 0], mats[q, 1]], axis=1)
                y = jnp.dot(low, both, preferred_element_type=F32)
            out = out + jnp.where(rows == 2 * q, y[:, :states], 0.0)
            out = out + jnp.where(rows == 2 * q + 1, y[:, states:], 0.0)
        return out * (1.0 / jnp.max(v, axis=-1, keepdims=True)) if level else out

    def carry(from_first, starts, arrivals, outs, k, back, g):
        side = -1 if back else 1
        start, arrived, out = starts.at[g], arrivals.at[g], outs.at[g]

        def send(step):
            to = jnp.clip(me + side * step, 0, n - 1)
            return pltpu.make_async_remote_copy(
                out, arrived, ssem.at[g, k, step - 1], rsem.at[g, k],
                device_id={"seq": to, "cell": jnp.where(from_first == 1, near, cell)},
                device_id_type=MESH,
            )

        relayed = relays.at[g, k]
        send_relay = pltpu.make_async_remote_copy(
            out, relayed, ls_sem.at[g, k], lr_sem.at[g, k],
            device_id={"seq": jnp.clip(me + side, 0, n - 1), "cell": near}, device_id_type=MESH,
        )
        odd = from_first % 2 == 1
        hops = jnp.logical_and(odd, from_first >= 3)
        sends = jnp.logical_and(hops, from_first < n - 1)
        turns = jnp.logical_and(from_first == 1, n > 2)
        twice = jnp.logical_and(odd, from_first < n - 2)

        def lead():
            @pl.when(from_first == 0)
            def _():
                start[...] = jnp.ones((CELLS, states), F32)

            @pl.when(jnp.logical_and(from_first == 0, n > 1))
            def _():
                v = jnp.ones((CELLS, states), F32)
                for node in (2 * count - 3, 2 * count - 4) if back else (2 * count - 4, 2 * count - 3):
                    v = through(v, tree_ref.at[g, node], diag_ref[g, node], back)
                out[...] = v
                if n > 2:
                    send_relay.start()
                send(1).start()

        def run():
            @pl.when(turns)
            def _():
                for copy in send_near(g):
                    copy.wait_recv()
                send_relay.wait_recv()
                out[...] = through(relayed[...], twin_ref.at[g], town_ref[g], back)
                send(2).start()
                send(1).start()

            @pl.when(from_first > 0)
            def _():
                send(1).wait_recv()

            @pl.when(jnp.logical_and(from_first > 0, jnp.logical_not(hops)))
            def _():
                start[...] = arrived[...]

            @pl.when(hops)
            def _():
                for copy in send_root(g):
                    copy.wait_recv()
                start[...] = through(arrived[...], next_ref.at[g], nown_ref[g], back)

            @pl.when(sends)
            def _():
                out[...] = through(start[...], root_ref.at[g], rown_ref[g], back)
                send(1).start()

            @pl.when(jnp.logical_and(twice, hops))
            def _():
                send(2).start()

        def finish():
            @pl.when(jnp.logical_or(jnp.logical_or(sends, turns), jnp.logical_and(from_first == 0, n > 1)))
            def _():
                send(1).wait_send()

            @pl.when(jnp.logical_and(from_first == 0, n > 2))
            def _():
                send_relay.wait_send()

            @pl.when(twice)
            def _():
                send(2).wait_send()

        return lead, run, finish

    def sweep(g, back, last):
        def step_through(v, node):
            return through(v, tree_ref.at[g, node], diag_ref[g, node], back, False)

        edge = count - 1 if back else 0
        chunk = {edge: win[g] if back else vin[g]}
        width = count // 2
        base = 2 * count - 4
        while width >= 1:
            for k in range(0, count, 2 * width):
                if back:
                    end = k + 2 * width - 1
                    chunk[end - width] = step_through(chunk[end], base + end // width)
                else:
                    chunk[k + width] = step_through(chunk[k], base + k // width)
            width //= 2
            if width:
                base -= count // width
        for k in range(count):
            st_ref[g, pl.ds(k * CELLS, CELLS), :] = chunk[k]

        def advance(v, ref, p):
            stacked = jnp.concatenate([v[:, :states], v[:, states:]], axis=0).astype(BF16)
            y = jnp.dot(stacked, ref[p], preferred_element_type=F32)
            y = jnp.concatenate([y[:count, :states], y[count:, states:]], axis=1)
            return y + v * own_ref[p]

        def emit(q, j, v):
            p = WIDTH * g + q
            joint = jnp.log(v) + kept_ref[p, j]
            joint = joint - wide_tops(joint)
            result = jnp.maximum(joint - jnp.log(wide_sums(jnp.exp(joint))), -30.0)
            for h in range(2):
                out_ref[2 * p + h, pl.ds(j, count, stride=SUB), :] = result[
                    :, h * states : (h + 1) * states
                ]

        state = [
            jnp.concatenate(
                [st_ref[g, pl.ds(2 * q + h, count, stride=CELLS), :] for h in range(2)], axis=1
            )
            for q in range(WIDTH)
        ]
        for step in range(SUB):
            j = SUB - 1 - step if back else step
            for q in range(WIDTH):
                p = WIDTH * g + q
                v = state[q]
                if not back or step < SUB - 1:
                    f = rates(p, j)
                    if step % (SUB // 2) == 0:
                        f = f * (1.0 / wide_tops(v))
                    if back:
                        state[q] = advance(v * f, flip_ref, p)
                    else:
                        state[q] = advance(v, off_ref, p) * f
                v = v if back else state[q]
                if last:
                    emit(q, j, v)
                else:
                    kept_ref[p, j] = jnp.log(v)

    carries = [
        (
            carry(me, vin, vgot, vout, 0, False, g),
            carry(n - 1 - me, win, wgot, wout, 1, True, g),
        )
        for g in range(groups)
    ]
    for g in range(groups):
        chain(g)
        for part in carries[g]:
            part[0]()
    early = 2 * me < n
    late = jnp.logical_not(early)
    for last in (False, True):
        for g in range(groups):
            for k, when in ((0, early), (1, late)):
                way = 1 - k if last else k

                @pl.when(when)
                def _():
                    carries[g][way][1]()
                    sweep(g, way == 1, last)

    for g in range(groups):
        for part in carries[g]:
            part[2]()

    @pl.when(swaps)
    def _():
        for g in range(groups):
            for copy in send_near(g):
                copy.wait_send()

    @pl.when(gives)
    def _():
        for g in range(groups):
            for copy in send_root(g):
                copy.wait_send()

    @pl.when(me < n - 1)
    def _():
        upward.wait_send()

    @pl.when(me > 0)
    def _():
        downward.wait_send()

    for layer in range(layers):
        send_conv(layer).wait_send()
        send_hidden(layer).wait_send()
        for k in range(3):
            send_weight(layer, k).wait_send()


def per_device(dna_bases, stem_weight, conv_weight, proj_weight, emission_head_weight, transitions):
    bins = dna_bases.shape[0] // BIN_BP
    cells, _, states = emission_head_weight.shape
    layers, held, taps, wide = conv_weight.shape
    padded = pl.cdiv(2 * held, 256) * 256
    count = bins // SUB
    groups = cells // 2 // WIDTH
    n = lax.axis_size("seq")
    assert layers == 2 and HALO == layers * MARGIN and MARGIN >= BASE_DILATION * 2 ** (layers - 1)
    assert lax.axis_size("cell") == 4 and 2 * WIDTH <= CELLS and cells % (2 * WIDTH) == 0 and (n == 1 or n % 2 == 0)
    vmem = pl.BlockSpec(memory_space=pltpu.VMEM)
    hbm = pl.BlockSpec(memory_space=pl.ANY)
    vec = pltpu.VMEM((groups, CELLS, states), F32)
    root = pltpu.VMEM((groups, WIDTH, 2, states, states), BF16)
    dma = pltpu.SemaphoreType.DMA
    square = (cells // 2, states, 2 * states)
    row = (cells // 2, 1, 2 * states)
    hidden = [pltpu.VMEM((bins + 2 * (HALO - (k + 1) * MARGIN), padded), BF16) for k in range(layers)]
    return pl.pallas_call(
        crf_kernel,
        name="crf",
        out_shape=jax.ShapeDtypeStruct((cells, bins, states), F32),
        in_specs=[hbm] * 6,
        out_specs=vmem,
        scratch_shapes=[
            pltpu.VMEM((bins, BIN_BP), jnp.int32),
            pltpu.VMEM(stem_weight.shape, BF16),
            pltpu.VMEM((layers, taps, padded, wide), BF16),
            pltpu.VMEM(emission_head_weight.shape, BF16),
            pltpu.VMEM(transitions.shape, F32),
            dma((2 * layers + 4,)),
            pltpu.VMEM((2 * HALO, BIN_BP), jnp.int32),
            pltpu.VMEM((layers, 2, padded, wide), BF16),
            hidden[0], hidden[0], hidden[1], hidden[1],
            dma((2,)), dma((2,)), dma((layers,)), dma((layers,)),
            dma((layers, 3)), dma((layers, 3)), dma((layers,)), dma((layers,)),
            pltpu.VMEM((bins, wide), BF16),
            pltpu.VMEM((cells, bins, states), F32),
            pltpu.VMEM(square, F32),
            pltpu.VMEM(square, BF16),
            pltpu.VMEM(square, BF16),
            pltpu.VMEM(row, F32),
            pltpu.VMEM(row, F32),
            pltpu.VMEM((groups, 2 * count - 2, WIDTH, 2, states, states), BF16),
            pltpu.VMEM((groups, 2 * count - 2, CELLS, states), F32),
            root, vec, root, vec,
            dma((groups, 2)), dma((groups, 2)),
            root, vec, dma((groups, 2)), dma((groups, 2)),
            pltpu.VMEM((groups, 2, CELLS, states), F32), dma((groups, 2)), dma((groups, 2)),
            vec, vec, vec, vec, vec, vec,
            pltpu.VMEM((groups, count * CELLS, states), F32),
            pltpu.VMEM((cells // 2, SUB, count, 2 * states), F32),
            dma((groups, 2, 2)), dma((groups, 2)),
        ],
        compiler_params=pltpu.CompilerParams(
            collective_id=1, has_side_effects=True, vmem_limit_bytes=VMEM_LIMIT
        ),
    )(
        dna_bases.reshape(bins, BIN_BP),
        stem_weight,
        conv_weight.transpose(0, 2, 1, 3),
        proj_weight,
        emission_head_weight,
        transitions,
    )


def solution(mesh):
    placed = (
        P(("groups", "seq")),
        P(),
        P(None, "cell", None, None),
        P(None, "cell", None),
        P("cell", None, None),
        P("cell", None, None),
    )
    return jax.shard_map(
        per_device,
        mesh=mesh,
        in_specs=placed,
        out_specs=P("cell", ("groups", "seq"), None),
        check_vma=False,
    )
```

```python
import functools

import jax
import jax.numpy as jnp
from jax import lax
from jax.experimental import pallas as pl
from jax.experimental.pallas import tpu as pltpu
from jax.sharding import PartitionSpec as P

BIN_BP = 128
BASE_DILATION = 4
SUB = 8
HALO = 16
MARGIN = 8
WIDTH = 2
CELLS = 8
VMEM_LIMIT = 54800 << 10
MESH = pl.DeviceIdType.MESH
F32 = jnp.float32
BF16 = jnp.bfloat16


def tops(x):
    m = jnp.max(x, axis=-2, keepdims=True)
    return wide_tops(m)


def wide_tops(m):
    half = m.shape[-1] // 2
    shape = m.shape[:-1] + (half,)
    left = jnp.max(m[..., :half], axis=-1, keepdims=True)
    right = jnp.max(m[..., half:], axis=-1, keepdims=True)
    return jnp.concatenate([jnp.broadcast_to(left, shape), jnp.broadcast_to(right, shape)], axis=-1)


def wide_sums(x):
    half = x.shape[-1] // 2
    shape = x.shape[:-1] + (half,)
    left = jnp.sum(x[..., :half], axis=-1, keepdims=True)
    right = jnp.sum(x[..., half:], axis=-1, keepdims=True)
    return jnp.concatenate([jnp.broadcast_to(left, shape), jnp.broadcast_to(right, shape)], axis=-1)


def two_blocks(x):
    half = x.shape[1] // 2
    zero = jnp.zeros((x.shape[0], half), x.dtype)
    return jnp.concatenate(
        [
            jnp.concatenate([x[:, :half], zero], axis=1),
            jnp.concatenate([zero, x[:, half:]], axis=1),
        ],
        axis=0,
    )


def rms(v):
    return v * lax.rsqrt(jnp.mean(v * v, axis=-1, keepdims=True) + 1e-06)


def crf_kernel(
    bases_hbm, stem_hbm, conv_hbm, proj_hbm, head_hbm, trans_hbm, out_ref,
    bases_ref, stem_ref, conv_ref, head_ref, trans_ref, lsem,
    wide_ref, wts_ref, mine0, got0, mine1, got1,
    hs_sem, hr_sem, cs_sem, cr_sem, ws_sem, wr_sem, gs_sem, gr_sem, feat_ref,
    f_ref, trn_ref, off_ref, flip_ref, own_ref, peak_ref, tree_ref, diag_ref,
    root_ref, rown_ref, next_ref, nown_ref, ms_sem, mr_sem,
    twin_ref, town_ref, xs_sem, xr_sem, relays, ls_sem, lr_sem,
    vin, win, vgot, wgot, vout, wout, st_ref, kept_ref, ssem, rsem,
):
    cells, states = head_ref.shape[0], head_ref.shape[2]
    bins = feat_ref.shape[0]
    layers, taps = conv_ref.shape[:2]
    held, padded, wide = conv_hbm.shape[2], conv_ref.shape[2], conv_ref.shape[3]
    count = bins // SUB
    n = lax.axis_size("seq")
    me = lax.axis_index("seq")
    cell = lax.axis_index("cell")
    near = cell + 1 - 2 * (cell % 2)
    far = (cell + 2) % 4
    diag = (near + 2) % 4
    first, second = pl.ds(0, held), pl.ds(held, held)

    pairs = [(bases_hbm, bases_ref)]
    pairs += [(proj_hbm.at[k], wts_ref.at[k, 0, first]) for k in range(layers)]
    pairs += [(conv_hbm.at[k], conv_ref.at[k, :, first]) for k in range(layers)]
    pairs += [(stem_hbm, stem_ref), (trans_hbm, trans_ref), (head_hbm, head_ref)]
    loads = [pltpu.make_async_copy(a, b, lsem.at[i]) for i, (a, b) in enumerate(pairs)]
    for load in loads:
        load.start()
    base_load, proj_loads, conv_loads = loads[0], loads[1 : layers + 1], loads[layers + 1 : -3]
    stem_load, trans_load, head_load = loads[-3:]

    barrier = pltpu.get_barrier_semaphore()
    for peer in (near, far, diag):
        pl.semaphore_signal(barrier, inc=1, device_id={"cell": peer}, device_id_type=MESH)
    for step in (-1, 1):

        @pl.when(jnp.logical_and(me + step >= 0, me + step < n))
        def _():
            pl.semaphore_signal(
                barrier, inc=1, device_id={"seq": me + step, "cell": near}, device_id_type=MESH
            )

    rown_ref[...] = jnp.ones_like(rown_ref)
    diag_ref[...] = jnp.ones_like(diag_ref)
    extra = padded - 2 * held
    if extra:
        for layer in range(layers):
            conv_ref[layer, :, pl.ds(2 * held, extra), :] = jnp.zeros((taps, extra, wide), BF16)
            wts_ref[layer, :, pl.ds(2 * held, extra), :] = jnp.zeros((2, extra, wide), BF16)
    base_load.wait()
    inner = jnp.logical_and(me > 0, me < n - 1)
    pl.semaphore_wait(barrier, jnp.where(inner, 5, 4 if n > 1 else 3))

    upward = pltpu.make_async_remote_copy(
        bases_ref.at[pl.ds(bins - HALO, HALO)], wide_ref.at[pl.ds(0, HALO)],
        hs_sem.at[0], hr_sem.at[0],
        device_id={"seq": jnp.minimum(me + 1, n - 1), "cell": near}, device_id_type=MESH,
    )
    downward = pltpu.make_async_remote_copy(
        bases_ref.at[pl.ds(0, HALO)], wide_ref.at[pl.ds(HALO, HALO)],
        hs_sem.at[1], hr_sem.at[1],
        device_id={"seq": jnp.maximum(me - 1, 0), "cell": near}, device_id_type=MESH,
    )

    @pl.when(me < n - 1)
    def _():
        upward.start()

    @pl.when(me > 0)
    def _():
        downward.start()

    def send_conv(layer):
        return pltpu.make_async_remote_copy(
            conv_ref.at[layer, :, first], conv_ref.at[layer, :, second],
            cs_sem.at[layer], cr_sem.at[layer],
            device_id={"cell": near}, device_id_type=MESH,
        )

    def send_weight(layer, k):
        source = wts_ref.at[layer, 1 if k == 2 else 0, first]
        target = wts_ref.at[layer, 0 if k == 0 else 1, first if k == 1 else second]
        return pltpu.make_async_remote_copy(
            source, target, ws_sem.at[layer, k], wr_sem.at[layer, k],
            device_id={"cell": diag if k == 1 else near}, device_id_type=MESH,
        )

    mine, got = (mine0, mine1), (got0, got1)

    def send_hidden(layer):
        return pltpu.make_async_remote_copy(
            mine[layer], got[layer], gs_sem.at[layer], gr_sem.at[layer],
            device_id={"cell": diag}, device_id_type=MESH,
        )

    for layer in range(layers):
        proj_loads[layer].wait()
        if layer == 0:
            send_weight(layer, 1).start()
        conv_loads[layer].wait()
        send_conv(layer).start()
        send_weight(layer, 0).start()

    states_sq = (states, 2 * states)
    eye = lax.broadcasted_iota(jnp.int32, states_sq, 0) == lax.broadcasted_iota(
        jnp.int32, states_sq, 1
    ) % states

    def prepare(p, _):
        raw = jnp.concatenate([trans_ref[2 * p], trans_ref[2 * p + 1]], axis=1)
        peak = jnp.max(raw, axis=0, keepdims=True)
        t = jnp.exp(raw - peak)
        off = jnp.where(eye, 0.0, t)
        peak_ref[p] = peak
        own_ref[p] = jnp.sum(jnp.where(eye, t, 0.0), axis=0, keepdims=True)
        trn_ref[p] = t
        off_ref[p] = off.astype(BF16)
        flip_ref[p] = jnp.concatenate([off[:, :states].T, off[:, states:].T], axis=1).astype(BF16)
        return 0

    trans_load.wait()
    lax.fori_loop(0, cells // 4, prepare, 0)

    columns = lax.broadcasted_iota(jnp.int32, (BIN_BP, 4 * BIN_BP), 1)
    spread = (columns // 4 == lax.broadcasted_iota(jnp.int32, columns.shape, 0)).astype(BF16)
    stem_load.wait()

    @pl.when(me > 0)
    def _():
        upward.wait_recv()

    @pl.when(me == 0)
    def _():
        wide_ref[pl.ds(0, HALO), :] = jnp.zeros((HALO, BIN_BP), jnp.int32)

    @pl.when(me < n - 1)
    def _():
        downward.wait_recv()

    @pl.when(me == n - 1)
    def _():
        wide_ref[pl.ds(HALO, HALO), :] = jnp.zeros((HALO, BIN_BP), jnp.int32)

    bases = jnp.concatenate(
        [wide_ref[pl.ds(0, HALO), :], bases_ref[...], wide_ref[pl.ds(HALO, HALO), :]], axis=0
    )
    repeated = jnp.dot(
        bases.astype(F32).astype(BF16), spread, preferred_element_type=F32
    )
    which = (lax.broadcasted_iota(jnp.int32, repeated.shape, 1) % 4).astype(F32)
    one_hot = jnp.where(repeated == which, 1.0, 0.0).astype(BF16)
    residual = jnp.dot(one_hot, stem_ref[...], preferred_element_type=F32).astype(BF16).astype(F32)
    for layer in range(layers):
        dilation = BASE_DILATION * 2**layer
        rows_in = residual.shape[0]
        place = lax.broadcasted_iota(jnp.int32, residual.shape, 0) + (
            me * bins - (rows_in - bins) // 2
        )
        inside = jnp.logical_and(place >= 0, place < n * bins)
        conv_in = jnp.where(inside, jax.nn.gelu(rms(residual)), 0.0).astype(BF16)
        send_conv(layer).wait_recv()
        tap = [
            lax.dot_general(
                conv_in, conv_ref[layer, k], (((1,), (1,)), ((), ())), preferred_element_type=F32
            )
            for k in range(taps)
        ]
        conv_out = (
            pltpu.roll(tap[0], dilation, 0) + tap[1] + pltpu.roll(tap[2], rows_in - dilation, 0)
        )[MARGIN : rows_in - MARGIN]
        hidden = jax.nn.gelu(conv_out).astype(BF16)
        mine[layer][...] = hidden
        send_hidden(layer).start()
        if layer + 1 < layers:
            send_weight(layer + 1, 1).start()
        send_weight(layer, 1).wait_recv()
        send_weight(layer, 2).start()
        send_weight(layer, 0).wait_recv()
        if layer == 0:
            lax.fori_loop(cells // 4, cells // 2, prepare, 0)
        send_weight(layer, 2).wait_recv()
        send_hidden(layer).wait_recv()
        residual = residual[MARGIN : rows_in - MARGIN] + jnp.dot(
            jnp.concatenate([hidden, got[layer][...]], axis=1),
            wts_ref[layer].reshape(2 * padded, wide),
            preferred_element_type=F32,
        )
    feat_ref[...] = rms(residual).astype(BF16)
    head_load.wait()

    even = me % 2 == 0
    gives = jnp.logical_or(
        jnp.logical_and(even, me >= 2), jnp.logical_and(jnp.logical_not(even), me <= n - 3)
    )
    beside = jnp.minimum(me + 1 - 2 * (me % 2), n - 1)
    groups = cells // 2 // WIDTH

    def send_root(g):
        return [
            pltpu.make_async_remote_copy(
                a.at[g], b.at[g], ms_sem.at[g, i], mr_sem.at[g, i],
                device_id={"seq": beside}, device_id_type=MESH,
            )
            for i, (a, b) in enumerate([(root_ref, next_ref), (rown_ref, nown_ref)])
        ]

    swaps = jnp.logical_and(jnp.logical_or(me == 1, me == n - 2), n > 2)

    def send_near(g):
        return [
            pltpu.make_async_remote_copy(
                a.at[g], b.at[g], xs_sem.at[g, i], xr_sem.at[g, i],
                device_id={"cell": near}, device_id_type=MESH,
            )
            for i, (a, b) in enumerate([(root_ref, twin_ref), (rown_ref, town_ref)])
        ]

    def rates(p, j):
        return jnp.concatenate(
            [f_ref[2 * p + h, pl.ds(j, count, stride=SUB), :] for h in range(2)], axis=1
        )

    def chain(g):
        group = [WIDTH * g + q for q in range(WIDTH)]
        for p in group:
            weight = jnp.concatenate([head_ref[2 * p], head_ref[2 * p + 1]], axis=1)
            e = jnp.dot(feat_ref[...], weight, preferred_element_type=F32) + peak_ref[p]
            f = jnp.exp(e - wide_tops(e))
            f_ref[2 * p] = f[:, :states]
            f_ref[2 * p + 1] = f[:, states:]
        blocks = [two_blocks(off_ref[p]) for p in group]
        xs = [trn_ref[p][None] * rates(p, 0)[:, None, :] for p in group]
        for j in range(1, SUB):
            for q, p in enumerate(group):
                x = xs[q]
                r = rates(p, j)
                h = r * own_ref[p]
                y = jnp.dot(
                    x.astype(BF16).reshape(count * states, 2 * states),
                    blocks[q],
                    preferred_element_type=F32,
                ).reshape(x.shape)
                xs[q] = y * r[:, None, :] + x * h[:, None, :]
        nodes = [[(x[k], 1.0 / tops(x[k])) for k in range(count)] for x in xs]

        def parted(x):
            slanted = jnp.where(eye, x, 0.0)
            return (x - slanted).astype(BF16), jnp.sum(slanted, axis=0, keepdims=True)

        def joined(left, off, own):
            y = jnp.dot(left.astype(BF16), two_blocks(off), preferred_element_type=F32)
            return y + left * own

        place = 0
        width = count
        while width > 1:
            following = [[] for _ in range(WIDTH)]
            ends = []
            for q in range(WIDTH):
                for k, (x, scale) in enumerate(nodes[q]):
                    off, own = parted(x)
                    for h in range(2):
                        half = slice(h * states, (h + 1) * states)
                        tree_ref[g, place + k, q, h] = off[:, half]
                        diag_ref[g, place + k, pl.ds(2 * q + h, 1), :] = own[:, half]
                    if k % 2 == 0:
                        left, left_scale = x, scale
                    elif width == 2:
                        ends.append((left, off, own))
                    else:
                        y = joined(left, off, own)
                        y = y if scale is None else y * (left_scale * scale)
                        following[q].append((y, None))
            nodes = following
            place += width
            width //= 2

        @pl.when(jnp.logical_and(me > 0, me < n - 1))
        def _():
            for q in range(WIDTH):
                off, own = parted(joined(*ends[q]))
                for h in range(2):
                    half = slice(h * states, (h + 1) * states)
                    root_ref[g, q, h] = off[:, half]
                    rown_ref[g, pl.ds(2 * q + h, 1), :] = own[:, half]

        @pl.when(swaps)
        def _():
            for copy in send_near(g):
                copy.start()

        @pl.when(gives)
        def _():
            for copy in send_root(g):
                copy.start()

    rows = lax.broadcasted_iota(jnp.int32, (CELLS, states), 0)

    def through(v, mats, own, back, level=True):
        low = v.astype(BF16)
        out = v * own
        for q in range(WIDTH):
            if back:
                y = lax.dot_general(
                    low, mats[q].reshape(2 * states, states),
                    (((1,), (1,)), ((), ())), preferred_element_type=F32,
                )
            else:
                both = jnp.concatenate([mats[q, 0], mats[q, 1]], axis=1)
                y = jnp.dot(low, both, preferred_element_type=F32)
            out = out + jnp.where(rows == 2 * q, y[:, :states], 0.0)
            out = out + jnp.where(rows == 2 * q + 1, y[:, states:], 0.0)
        return out * (1.0 / jnp.max(v, axis=-1, keepdims=True)) if level else out

    def carry(from_first, starts, arrivals, outs, k, back, g):
        side = -1 if back else 1
        start, arrived, out = starts.at[g], arrivals.at[g], outs.at[g]

        def send(step):
            to = jnp.clip(me + side * step, 0, n - 1)
            return pltpu.make_async_remote_copy(
                out, arrived, ssem.at[g, k, step - 1], rsem.at[g, k],
                device_id={"seq": to, "cell": jnp.where(from_first == 1, near, cell)},
                device_id_type=MESH,
            )

        relayed = relays.at[g, k]
        send_relay = pltpu.make_async_remote_copy(
            out, relayed, ls_sem.at[g, k], lr_sem.at[g, k],
            device_id={"seq": jnp.clip(me + side, 0, n - 1), "cell": near}, device_id_type=MESH,
        )
        odd = from_first % 2 == 1
        hops = jnp.logical_and(odd, from_first >= 3)
        sends = jnp.logical_and(hops, from_first < n - 1)
        turns = jnp.logical_and(from_first == 1, n > 2)
        twice = jnp.logical_and(odd, from_first < n - 2)

        def lead():
            @pl.when(from_first == 0)
            def _():
                start[...] = jnp.ones((CELLS, states), F32)

            @pl.when(jnp.logical_and(from_first == 0, n > 1))
            def _():
                v = jnp.ones((CELLS, states), F32)
                for node in (2 * count - 3, 2 * count - 4) if back else (2 * count - 4, 2 * count - 3):
                    v = through(v, tree_ref.at[g, node], diag_ref[g, node], back)
                out[...] = v
                if n > 2:
                    send_relay.start()
                send(1).start()

        def run():
            @pl.when(turns)
            def _():
                for copy in send_near(g):
                    copy.wait_recv()
                send_relay.wait_recv()
                out[...] = through(relayed[...], twin_ref.at[g], town_ref[g], back)
                send(2).start()
                send(1).start()

            @pl.when(from_first > 0)
            def _():
                send(1).wait_recv()

            @pl.when(jnp.logical_and(from_first > 0, jnp.logical_not(hops)))
            def _():
                start[...] = arrived[...]

            @pl.when(hops)
            def _():
                for copy in send_root(g):
                    copy.wait_recv()
                start[...] = through(arrived[...], next_ref.at[g], nown_ref[g], back)

            @pl.when(sends)
            def _():
                out[...] = through(start[...], root_ref.at[g], rown_ref[g], back)
                send(1).start()

            @pl.when(jnp.logical_and(twice, hops))
            def _():
                send(2).start()

        def finish():
            @pl.when(jnp.logical_or(jnp.logical_or(sends, turns), jnp.logical_and(from_first == 0, n > 1)))
            def _():
                send(1).wait_send()

            @pl.when(jnp.logical_and(from_first == 0, n > 2))
            def _():
                send_relay.wait_send()

            @pl.when(twice)
            def _():
                send(2).wait_send()

        return lead, run, finish

    def sweep(g, back, last):
        def step_through(v, node):
            return through(v, tree_ref.at[g, node], diag_ref[g, node], back, False)

        edge = count - 1 if back else 0
        chunk = {edge: win[g] if back else vin[g]}
        width = count // 2
        base = 2 * count - 4
        while width >= 1:
            for k in range(0, count, 2 * width):
                if back:
                    end = k + 2 * width - 1
                    chunk[end - width] = step_through(chunk[end], base + end // width)
                else:
                    chunk[k + width] = step_through(chunk[k], base + k // width)
            width //= 2
            if width:
                base -= count // width
        for k in range(count):
            st_ref[g, pl.ds(k * CELLS, CELLS), :] = chunk[k]

        def advance(v, ref, p):
            stacked = jnp.concatenate([v[:, :states], v[:, states:]], axis=0).astype(BF16)
            y = jnp.dot(stacked, ref[p], preferred_element_type=F32)
            y = jnp.concatenate([y[:count, :states], y[count:, states:]], axis=1)
            return y + v * own_ref[p]

        def emit(q, j, v):
            p = WIDTH * g + q
            joint = jnp.log(v) + kept_ref[p, j]
            joint = joint - wide_tops(joint)
            result = jnp.maximum(joint - jnp.log(wide_sums(jnp.exp(joint))), -30.0)
            for h in range(2):
                out_ref[2 * p + h, pl.ds(j, count, stride=SUB), :] = result[
                    :, h * states : (h + 1) * states
                ]

        state = [
            jnp.concatenate(
                [st_ref[g, pl.ds(2 * q + h, count, stride=CELLS), :] for h in range(2)], axis=1
            )
            for q in range(WIDTH)
        ]
        for step in range(SUB):
            j = SUB - 1 - step if back else step
            for q in range(WIDTH):
                p = WIDTH * g + q
                v = state[q]
                if not back or step < SUB - 1:
                    f = rates(p, j)
                    if step == 0:
                        f = f * (1.0 / wide_tops(v))
                    if back:
                        state[q] = advance(v * f, flip_ref, p)
                    else:
                        state[q] = advance(v, off_ref, p) * f
                v = v if back else state[q]
                if last:
                    emit(q, j, v)
                else:
                    kept_ref[p, j] = jnp.log(v)

    carries = [
        (
            carry(me, vin, vgot, vout, 0, False, g),
            carry(n - 1 - me, win, wgot, wout, 1, True, g),
        )
        for g in range(groups)
    ]
    for g in range(groups):
        chain(g)
        for part in carries[g]:
            part[0]()
    early = 2 * me < n
    late = jnp.logical_not(early)
    for last in (False, True):
        for g in range(groups):
            for k, when in ((0, early), (1, late)):
                way = 1 - k if last else k

                @pl.when(when)
                def _():
                    carries[g][way][1]()
                    sweep(g, way == 1, last)

    for g in range(groups):
        for part in carries[g]:
            part[2]()

    @pl.when(swaps)
    def _():
        for g in range(groups):
            for copy in send_near(g):
                copy.wait_send()

    @pl.when(gives)
    def _():
        for g in range(groups):
            for copy in send_root(g):
                copy.wait_send()

    @pl.when(me < n - 1)
    def _():
        upward.wait_send()

    @pl.when(me > 0)
    def _():
        downward.wait_send()

    for layer in range(layers):
        send_conv(layer).wait_send()
        send_hidden(layer).wait_send()
        for k in range(3):
            send_weight(layer, k).wait_send()


def per_device(dna_bases, stem_weight, conv_weight, proj_weight, emission_head_weight, transitions):
    bins = dna_bases.shape[0] // BIN_BP
    cells, _, states = emission_head_weight.shape
    layers, held, taps, wide = conv_weight.shape
    padded = pl.cdiv(2 * held, 256) * 256
    count = bins // SUB
    groups = cells // 2 // WIDTH
    n = lax.axis_size("seq")
    assert layers == 2 and HALO == layers * MARGIN and MARGIN >= BASE_DILATION * 2 ** (layers - 1)
    assert lax.axis_size("cell") == 4 and 2 * WIDTH <= CELLS and cells % (2 * WIDTH) == 0 and (n == 1 or n % 2 == 0)
    vmem = pl.BlockSpec(memory_space=pltpu.VMEM)
    hbm = pl.BlockSpec(memory_space=pl.ANY)
    vec = pltpu.VMEM((groups, CELLS, states), F32)
    root = pltpu.VMEM((groups, WIDTH, 2, states, states), BF16)
    dma = pltpu.SemaphoreType.DMA
    square = (cells // 2, states, 2 * states)
    row = (cells // 2, 1, 2 * states)
    hidden = [pltpu.VMEM((bins + 2 * (HALO - (k + 1) * MARGIN), padded), BF16) for k in range(layers)]
    return pl.pallas_call(
        crf_kernel,
        name="crf",
        out_shape=jax.ShapeDtypeStruct((cells, bins, states), F32),
        in_specs=[hbm] * 6,
        out_specs=vmem,
        scratch_shapes=[
            pltpu.VMEM((bins, BIN_BP), jnp.int32),
            pltpu.VMEM(stem_weight.shape, BF16),
            pltpu.VMEM((layers, taps, padded, wide), BF16),
            pltpu.VMEM(emission_head_weight.shape, BF16),
            pltpu.VMEM(transitions.shape, F32),
            dma((2 * layers + 4,)),
            pltpu.VMEM((2 * HALO, BIN_BP), jnp.int32),
            pltpu.VMEM((layers, 2, padded, wide), BF16),
            hidden[0], hidden[0], hidden[1], hidden[1],
            dma((2,)), dma((2,)), dma((layers,)), dma((layers,)),
            dma((layers, 3)), dma((layers, 3)), dma((layers,)), dma((layers,)),
            pltpu.VMEM((bins, wide), BF16),
            pltpu.VMEM((cells, bins, states), F32),
            pltpu.VMEM(square, F32),
            pltpu.VMEM(square, BF16),
            pltpu.VMEM(square, BF16),
            pltpu.VMEM(row, F32),
            pltpu.VMEM(row, F32),
            pltpu.VMEM((groups, 2 * count - 2, WIDTH, 2, states, states), BF16),
            pltpu.VMEM((groups, 2 * count - 2, CELLS, states), F32),
            root, vec, root, vec,
            dma((groups, 2)), dma((groups, 2)),
            root, vec, dma((groups, 2)), dma((groups, 2)),
            pltpu.VMEM((groups, 2, CELLS, states), F32), dma((groups, 2)), dma((groups, 2)),
            vec, vec, vec, vec, vec, vec,
            pltpu.VMEM((groups, count * CELLS, states), F32),
            pltpu.VMEM((cells // 2, SUB, count, 2 * states), F32),
            dma((groups, 2, 2)), dma((groups, 2)),
        ],
        compiler_params=pltpu.CompilerParams(
            collective_id=1, has_side_effects=True, vmem_limit_bytes=VMEM_LIMIT
        ),
    )(
        dna_bases.reshape(bins, BIN_BP),
        stem_weight,
        conv_weight.transpose(0, 2, 1, 3),
        proj_weight,
        emission_head_weight,
        transitions,
    )


def solution(mesh):
    placed = (
        P(("groups", "seq")),
        P(),
        P(None, "cell", None, None),
        P(None, "cell", None),
        P("cell", None, None),
        P("cell", None, None),
    )
    return jax.shard_map(
        per_device,
        mesh=mesh,
        in_specs=placed,
        out_specs=P("cell", ("groups", "seq"), None),
        check_vma=False,
    )
```
